256 devices in a mesh: modes: 8 (over x_lo, y), atoms: 32 (over x_hi, z, core).
Axes of the slice: x: 4 (x_hi: 2, x_lo: 2; x = x_hi * 2 + x_lo), y: 4, z: 8, core: 2. Of those that a mesh axis runs over, the one named last changes fastest.
Arguments:
- left_modes: bfloat16 [3, 32768, 6144], P(None, 'atoms', 'modes'), may hold values from -6 to 6
- right_panel: bfloat16 [3, 32768, 256], P(None, 'atoms', 'modes'), may hold values from -6 to 6
- force_blocks: float32 [3, 3, 16, 32768], P(None, None, None, 'atoms'), may hold values from -0.875 to 0.875
- bond_vectors: float32 [3, 16, 32768], P(None, None, 'atoms'), may hold values from -1 to 1
- neighbours: int32 [16, 32768], P(None, 'atoms'), may hold values from 0 to 32767, as said below
- counts: int32 [32768], P('atoms'), may hold values from 1 to 16
- left_bins: int32 [6144], P(('modes', 'atoms')), may hold values from 1 to 32
- right_bins: int32 [256], replicated, may hold values from 1 to 32
Outputs:
- diffusivity: float32 [6144], P(('modes', 'atoms'))
The draws below stay inside these ranges and needn't reach their ends.
Inputs may be any that keep to these rules, and one draw needn't show every extreme that they name: neighbours[k, a] = (a + s) modulo 32768 with 1 <= |s| <= 256; some entry has |s| = 256.
All inputs are finite; a program needn't handle non-finite values.
Results may differ from the reference program's by a relative error of at most 0.00058.
Values may be sent and summed in bfloat16 or wider, within the bound.
No kernel may reach another device: no remote copies, remote signals or barrier semaphores. Data moves between devices by JAX's collectives and lax.ppermute only.
A program may use at most 128 MiB of HBM per device.

```python
import math
import jax
import jax.numpy as jnp
from jax import lax

PANEL = 256
K = 16
NBINS = 32
HALO = 256
ATOMS = 32768
LEFT = 6144


def draw_neighbours(key, part):
    key_size, key_sign, key_far = jax.random.split(jax.random.fold_in(key, 7), 3)
    distance = jax.random.randint(key_size, (K, ATOMS), 1, HALO + 1)
    direction_sign = jax.random.randint(key_sign, (K, ATOMS), 0, 2) * 2 - 1
    offsets = distance * direction_sign
    far_atoms = jax.random.randint(key_far, (2,), 0, ATOMS)
    offsets = offsets.at[0, far_atoms[0]].set(HALO)
    offsets = offsets.at[0, far_atoms[1]].set(-HALO)
    atom_ids = lax.broadcasted_iota(jnp.int32, (K, ATOMS), 1)
    return jnp.mod(atom_ids + offsets, ATOMS).astype(jnp.int32)


def set_ends(drawn, own_key, low, largest):
    spot = [jax.random.randint(jax.random.fold_in(own_key, axis), (), 0, length) for axis, length in enumerate(drawn.shape)]
    main_axis = drawn.shape.index(max(drawn.shape))
    beside = spot[:main_axis] + [(spot[main_axis] + 1) % drawn.shape[main_axis]] + spot[main_axis + 1:]
    return drawn.at[tuple(spot)].set(low).at[tuple(beside)].set(largest)


def with_spikes(array, own_key, source, target, parts, factor):
    owner, partner = [(jnp.arange(array.shape[position]) // (array.shape[position] // parts)).reshape([-1 if axis == position else 1 for axis in range(array.ndim)]) for position in (source, target)]
    chosen = jax.random.permutation(own_key, parts)[partner]
    strong = (owner == chosen) | (owner == (partner + parts // 2) % parts)
    return jnp.where(strong, factor * array, array)


def levels(rng, extent, pieces, low, top_value):
    def one(axis_at, blocks):
        steps = jax.random.uniform(jax.random.fold_in(jax.random.fold_in(rng, 6), axis_at), (blocks,), jnp.float32, low / len(pieces), top_value / len(pieces))
        return jnp.repeat(jnp.exp(steps), extent[axis_at] // blocks).reshape((-1,) + (1,) * (len(extent) - axis_at - 1))

    loudness = one(*pieces[0])
    for cut in pieces[1:]:
        loudness = loudness * one(*cut)
    return loudness


def bell_draw(own_key, dims, spread, most, cuts=(), kind=jnp.bfloat16):
    array = jax.random.normal(own_key, dims, jnp.float32) * spread
    if len(cuts) > 0:
        array = levels(own_key, dims, cuts, -0.22, 0.18) * array
    return jnp.clip(array, min=-most, max=most).astype(kind)


def noise_with(stream_key, extent, spread, most, cuts, heavy, kind=jnp.bfloat16):
    drawn = spread * jax.random.normal(stream_key, extent, jnp.float32)
    if cuts:
        drawn = drawn * levels(stream_key, extent, cuts, -0.22, 0.18)
    return jnp.clip(with_spikes(drawn, jax.random.fold_in(stream_key, 3), *heavy), -most, most).astype(kind)


def setup_inputs(seed: int = 0) -> dict:
    key_of = jax.random.split(jax.random.key(seed), 9)
    return {
        "left_modes": noise_with(key_of[0], (3, ATOMS, LEFT), 1.0, 6.0, ((1, 32), (2, 8)), (1, 2, 32, 2.75)),
        "right_panel": bell_draw(key_of[1], (3, ATOMS, PANEL), 1.0, 6.0, ((1, 32), (2, 8))),
        "force_blocks": bell_draw(key_of[2], (3, 3, K, ATOMS), (3 * K) ** -0.5, 0.875, ((3, 32),), jnp.float32),
        "bond_vectors": jnp.clip(jax.random.uniform(key_of[3], (3, K, ATOMS), jnp.float32, -1.0, 1.0) * levels(key_of[3], (3, K, ATOMS), ((2, 32),), -0.4, 0.0), -1.0, 1.0),
        "neighbours": draw_neighbours(jax.random.fold_in(key_of[8], 71), 0),
        "counts": set_ends(jax.random.randint(key_of[5], (ATOMS,), 1, K + 1), jax.random.fold_in(key_of[5], 1), 1, K).astype(jnp.int32),
        "left_bins": set_ends(jax.random.randint(key_of[6], (LEFT,), 1, NBINS + 1), jax.random.fold_in(key_of[6], 1), 1, NBINS).astype(jnp.int32),
        "right_bins": set_ends(jax.random.randint(key_of[7], (PANEL,), 1, NBINS + 1), jax.random.fold_in(key_of[7], 1), 1, NBINS).astype(jnp.int32),
    }


omega_step = 0.05
gamma = 0.1


def operator_blocks(force_blocks, bond_vectors, counts):
    slot_ids = lax.broadcasted_iota(jnp.int32, bond_vectors.shape[1:], 0)
    live_slot = (slot_ids < counts[None, :]).astype(jnp.float32)
    scaled = bond_vectors * live_slot[None]
    return (scaled[:, None, None, :, :] * force_blocks[None]).astype(jnp.bfloat16)


def reference(left_modes, right_panel, force_blocks, bond_vectors, neighbours, counts, left_bins, right_bins):
    blocks = operator_blocks(force_blocks, bond_vectors, counts)
    block_width = math.gcd(ATOMS, 256)
    starts = jnp.arange(ATOMS // block_width, dtype=jnp.int32) * block_width

    def one_block(start_row):
        near_index = lax.dynamic_slice_in_dim(neighbours, start_row, block_width, 1)
        nearby = right_panel[:, near_index, :].astype(jnp.float32)
        coefficient = lax.dynamic_slice_in_dim(blocks, start_row, block_width, 4).astype(jnp.float32)
        return jnp.einsum('xcdkb,dkbj->xcbj', coefficient, nearby).astype(jnp.bfloat16)

    stacked = lax.map(one_block, starts)
    flux_all = jnp.moveaxis(stacked, 0, 2).reshape(3, 3 * ATOMS, PANEL)
    left_flat = left_modes.reshape(3 * ATOMS, LEFT)
    squares = jnp.zeros((LEFT, PANEL), jnp.float32)
    for direction in range(3):
        coupling = lax.dot_general(left_flat, flux_all[direction], (((0,), (0,)), ((), ())), preferred_element_type=jnp.float32)
        squares = squares + coupling * coupling
    omega_left = omega_step * left_bins.astype(jnp.float32)
    omega_right = omega_step * right_bins.astype(jnp.float32)
    freq_gap = omega_left[:, None] - omega_right[None, :]
    weight = gamma * gamma / (freq_gap * freq_gap + gamma * gamma)
    weight = weight * (omega_left[:, None] + omega_right[None, :]) ** 2 / (4.0 * omega_left[:, None] * omega_right[None, :])
    return 4.0 * jnp.sum(weight * squares, axis=1) / (ATOMS * PANEL)
```

```python
import functools
import jax, jax.numpy as jnp
from jax import lax
from jax.experimental import pallas as pl
from jax.experimental.pallas import tpu as pltpu

B = 256
G = 16
NT = (((1,), (1,)), ((), ()))


def swap_tile(t):
    row = lax.broadcasted_iota(jnp.int32, (8, 128), 0)
    col = lax.broadcasted_iota(jnp.int32, (8, 128), 1) // G
    for s in (4, 2, 1):
        low_row = (row & s) == 0
        same = (row & s) == (col & s)
        up = pltpu.roll(pltpu.roll(t, 8 - s, 0), G * s, 1)
        down = up if s == 4 else pltpu.roll(pltpu.roll(t, s, 0), 128 - G * s, 1)
        t = jnp.where(same, t, jnp.where(low_row, up, down))
    return t


def prep_kernel(first_ref, force_ref, bond_ref, nbr_ref, counts_ref, yop_ref, yidx_ref, *, total_atoms):
    step = pl.program_id(0)
    cnt = counts_ref[...]
    first = first_ref[0]
    block_start = (step // 2) * B
    for h in range(2):
        ids = lax.broadcasted_iota(jnp.int32, (8, 128), 0) + 8 * h
        live = ids < cnt
        e = nbr_ref[8 * h:8 * h + 8, :] - first + B
        e = jnp.where(e < 0, e + total_atoms, e)
        e = jnp.where(e >= total_atoms, e - total_atoms, e)
        yidx_ref[:, 128 * h:128 * h + 128] = swap_tile((e - block_start).astype(jnp.float32)).astype(jnp.int32)
        for x in range(3):
            scaled = jnp.where(live, bond_ref[x, 8 * h:8 * h + 8, :], 0.0)
            for c in range(3):
                for d in range(3):
                    op = (scaled * force_ref[c, d, 8 * h:8 * h + 8, :]).astype(jnp.bfloat16).astype(jnp.float32)
                    yop_ref[(x * 3 + c) * 3 + d, :, 128 * h:128 * h + 128] = swap_tile(op)


def prep(first, force, bond, nbr, counts, total_atoms):
    atoms = nbr.shape[1]
    steps = atoms // 128
    groups = atoms // G
    return pl.pallas_call(
        functools.partial(prep_kernel, total_atoms=total_atoms),
        grid_spec=pltpu.PrefetchScalarGridSpec(
            num_scalar_prefetch=1,
            grid=(steps,),
            in_specs=[
                pl.BlockSpec((3, 3, 16, 128), lambda s, f: (0, 0, 0, s)),
                pl.BlockSpec((3, 16, 128), lambda s, f: (0, 0, s)),
                pl.BlockSpec((16, 128), lambda s, f: (0, s)),
                pl.BlockSpec((1, 128), lambda s, f: (0, s)),
            ],
            out_specs=[
                pl.BlockSpec((27, 8, 256), lambda s, f: (0, s, 0)),
                pl.BlockSpec((8, 256), lambda s, f: (s, 0)),
            ],
        ),
        out_shape=[
            jax.ShapeDtypeStruct((27, groups, 256), jnp.float32),
            jax.ShapeDtypeStruct((groups, 256), jnp.int32),
        ],
        name="prep",
    )(first, force, bond, nbr, counts)


def turn_kernel(left_ref, out_ref):
    out_ref[0] = left_ref[0].T


def turn_left(left):
    _, atoms, modes = left.shape
    return pl.pallas_call(
        turn_kernel,
        grid=(atoms // B, 3),
        in_specs=[pl.BlockSpec((1, B, modes), lambda b, c: (c, b, 0))],
        out_specs=pl.BlockSpec((1, modes, B), lambda b, c: (b, 0, c)),
        out_shape=jax.ShapeDtypeStruct((atoms // B, modes, 3 * B), jnp.bfloat16),
        name="turn",
    )(left)


def flux_kernel(rt_ref, yidx_ref, yop_ref, leftT_ref, acc_ref, oh, near, ct, flux, *, J, unroll):
    step = pl.program_id(0)
    rows = lax.broadcasted_iota(jnp.int32, (B, 256), 0)
    own = (lax.broadcasted_iota(jnp.int32, (G, 256), 0)) == (lax.broadcasted_iota(jnp.int32, (G, 256), 1) & (G - 1))

    def one_group(g):
        u = 0
        idx = yidx_ref[pl.ds(g, 1), :]
        for t in range(3):
            oh[t * B:(t + 1) * B, :] = jnp.where(rows == idx - t * B, 1.0, 0.0).astype(jnp.bfloat16)
        for d in range(3):
            n = jnp.dot(rt_ref[d], oh[...], preferred_element_type=jnp.float32)
            near[:, d * 256:(d + 1) * 256] = n.astype(jnp.bfloat16)
        for xc in range(9):
            for d in range(3):
                v = yop_ref[xc * 3 + d, pl.ds(g, 1), :]
                ct[xc * G:(xc + 1) * G, d * 256:(d + 1) * 256] = jnp.where(own, v, 0.0).astype(jnp.bfloat16)
        fl = lax.dot_general(ct[...], near[...], NT, preferred_element_type=jnp.float32).astype(jnp.bfloat16)
        a0 = pl.multiple_of(g * G, G)
        for x in range(3):
            for c in range(3):
                xc = x * 3 + c
                flux[pl.ds(pl.multiple_of(c * B + a0, G), G), x * J:(x + 1) * J] = fl[xc * G:(xc + 1) * G, :]

    def body(i, carry):
        for u in range(unroll):
            one_group(i * unroll + u)
        return carry

    lax.fori_loop(0, B // G // unroll, body, 0)
    part = jnp.dot(leftT_ref[0], flux[...], preferred_element_type=jnp.float32)

    @pl.when(step == 0)
    def _():
        acc_ref[...] = part

    @pl.when(step != 0)
    def _():
        acc_ref[...] += part


def flux_call(ext, yidx, yop, leftT, unroll=1):
    J = ext.shape[1]
    nb, modes, _ = leftT.shape
    return pl.pallas_call(
        functools.partial(flux_kernel, J=J, unroll=unroll),
        grid=(nb,),
        in_specs=[
            pl.BlockSpec((pl.Element(3), pl.Element(J), pl.Element(3 * B)), lambda b: (0, 0, b * B)),
            pl.BlockSpec((G, 256), lambda b: (b, 0)),
            pl.BlockSpec((27, G, 256), lambda b: (0, b, 0)),
            pl.BlockSpec((1, modes, 3 * B), lambda b: (b, 0, 0)),
        ],
        out_specs=pl.BlockSpec((modes, 3 * J), lambda b: (0, 0)),
        out_shape=jax.ShapeDtypeStruct((modes, 3 * J), jnp.float32),
        scratch_shapes=[
            pltpu.VMEM((3 * B, 256), jnp.bfloat16),
            pltpu.VMEM((J, 768), jnp.bfloat16),
            pltpu.VMEM((9 * G, 768), jnp.bfloat16),
            pltpu.VMEM((3 * B, 3 * J), jnp.bfloat16),
        ],
        name="flux",
    )(ext, yidx, yop, leftT)


omega_step = 0.05
gamma = 0.1


def per_device(left_modes, right_panel, force_blocks, bond_vectors, neighbours, counts, left_bins, right_bins):
    atoms_dev = right_panel.shape[1]
    cols = right_panel.shape[2]
    modes_dev = left_modes.shape[2]
    n_modes = lax.axis_size("modes")
    n_atoms = lax.axis_size("atoms")
    total_atoms = atoms_dev * n_atoms
    me = lax.axis_index("atoms")
    mode = lax.axis_index("modes")
    ny = n_modes // 2

    def y_from(a, k):
        return lax.ppermute(a, "modes", [((i // ny) * ny + (i % ny + k) % ny, i) for i in range(n_modes)])

    def other_x(a):
        return lax.ppermute(a, "modes", [(i, (i + ny) % n_modes) for i in range(n_modes)])

    own = jnp.swapaxes(right_panel, 1, 2)
    near_y = [own] + [y_from(own, k) for k in range(1, ny)]
    half = jnp.concatenate(near_y, axis=1)
    whole = jnp.concatenate([half, other_x(half)], axis=1)
    up = [(i, (i + 1) % n_atoms) for i in range(n_atoms)]
    down = [(i, (i - 1) % n_atoms) for i in range(n_atoms)]
    low = lax.ppermute(whole[:, :, atoms_dev - B:], "atoms", up)
    high = lax.ppermute(whole[:, :, :B], "atoms", down)
    ext = jnp.concatenate([low, whole, high], axis=2)

    first = (me * atoms_dev).astype(jnp.int32).reshape(1)
    yop, yidx = prep(first, force_blocks, bond_vectors, neighbours, counts.reshape(1, -1), total_atoms)
    turned = turn_left(left_modes)
    part = flux_call(ext, yidx, yop, turned, 2)

    n_core = 2
    n_chip = n_atoms // n_core
    mine = modes_dev // n_atoms
    width = part.shape[1]
    part = part.reshape(n_chip, n_core, mine, width)
    core = me % n_core
    keep = lax.dynamic_index_in_dim(part, core, 1, keepdims=False)
    send = lax.dynamic_index_in_dim(part, 1 - core, 1, keepdims=False)
    got = lax.ppermute(send, "atoms", [(i, i ^ 1) for i in range(n_atoms)])
    chip = (keep + got).astype(jnp.bfloat16)
    groups = [[c + n_core * i for i in range(n_chip)] for c in range(n_core)]
    parts = lax.all_to_all(chip, "atoms", 0, 0, axis_index_groups=groups, tiled=True)
    total = jnp.sum(parts.astype(jnp.float32), axis=0).reshape(mine, 3, -1)
    squares = jnp.sum(total * total, axis=1)

    x_lo, y = mode // ny, mode % ny
    table = right_bins.reshape(2, ny, cols)
    table = jnp.where(x_lo == 0, table, table[::-1])
    table = lax.dynamic_slice_in_dim(jnp.concatenate([table, table], axis=1), y, ny, axis=1)
    omega_left = omega_step * left_bins.astype(jnp.float32)
    omega_right = omega_step * table.reshape(-1).astype(jnp.float32)
    freq_gap = omega_left[:, None] - omega_right[None, :]
    weight = gamma * gamma / (freq_gap * freq_gap + gamma * gamma)
    weight = weight * (omega_left[:, None] + omega_right[None, :]) ** 2 / (4.0 * omega_left[:, None] * omega_right[None, :])
    return 4.0 * jnp.sum(weight * squares, axis=1) / (total_atoms * n_modes * cols)


def solution(mesh):
    from jax.sharding import PartitionSpec as P

    return jax.shard_map(
        per_device,
        mesh=mesh,
        in_specs=(
            P(None, "atoms", "modes"),
            P(None, "atoms", "modes"),
            P(None, None, None, "atoms"),
            P(None, None, "atoms"),
            P(None, "atoms"),
            P("atoms"),
            P(("modes", "atoms")),
            P(),
        ),
        out_specs=P(("modes", "atoms")),
        check_vma=False,
    )
```

```python
import functools
import jax, jax.numpy as jnp
from jax import lax
from jax.experimental import pallas as pl
from jax.experimental.pallas import tpu as pltpu

REACH = 256
G = 16
T = 128
WIN = T + 2 * REACH
S = 2 * T
NT = (((1,), (1,)), ((), ()))


def cost(flops, moved):
    return pl.CostEstimate(flops=flops, bytes_accessed=moved, transcendentals=0)


def swap_tile(t):
    row = lax.broadcasted_iota(jnp.int32, (8, 128), 0)
    col = lax.broadcasted_iota(jnp.int32, (8, 128), 1) // G
    for s in (4, 2, 1):
        low_row = (row & s) == 0
        same = (row & s) == (col & s)
        up = pltpu.roll(pltpu.roll(t, 8 - s, 0), G * s, 1)
        down = up if s == 4 else pltpu.roll(pltpu.roll(t, s, 0), 128 - G * s, 1)
        t = jnp.where(same, t, jnp.where(low_row, up, down))
    return t


def turn_kernel(left_ref, out_ref):
    unit = lax.broadcasted_iota(jnp.int32, (S, S), 0) == lax.broadcasted_iota(jnp.int32, (S, S), 1)
    unit = jnp.where(unit, 1.0, 0.0).astype(jnp.bfloat16)
    for c in range(3):
        for t in range(left_ref.shape[2] // S):
            cols = slice(t * S, (t + 1) * S)
            turned = lax.dot_general(unit, left_ref[c, :, cols], NT, preferred_element_type=jnp.float32)
            out_ref[0, cols, c * S:(c + 1) * S] = turned.astype(jnp.bfloat16)


def turn_left(left):
    _, atoms, modes = left.shape
    return pl.pallas_call(
        turn_kernel,
        grid=(atoms // S,),
        in_specs=[pl.BlockSpec((3, S, modes), lambda b: (0, b, 0))],
        out_specs=pl.BlockSpec((1, modes, 3 * S), lambda b: (b, 0, 0)),
        out_shape=jax.ShapeDtypeStruct((atoms // S, modes, 3 * S), jnp.bfloat16),
        cost_estimate=cost(2 * left.size * S, 4 * left.size),
        name="turn",
    )(left)


def operator_kernel(first_ref, force_ref, bond_ref, nbr_ref, counts_ref, out_ref, rows, idx, hot, ct, *, total_atoms, unroll):
    step = pl.program_id(0)
    cnt = counts_ref[...]
    shift = first_ref[0] + step * T - REACH
    for h in range(2):
        lanes = slice(128 * h, 128 * h + 128)
        slots = slice(8 * h, 8 * h + 8)
        live = lax.broadcasted_iota(jnp.int32, (8, 128), 0) + 8 * h < cnt
        e = nbr_ref[slots, :] - shift
        e = jnp.where(e < 0, e + total_atoms, e)
        e = jnp.where(e >= total_atoms, e - total_atoms, e)
        idx[:, lanes] = swap_tile(e.astype(jnp.float32)).astype(jnp.int32)
        for x in range(3):
            scaled = jnp.where(live, bond_ref[x, slots, :], 0.0)
            for c in range(3):
                for d in range(3):
                    op = (scaled * force_ref[c, d, slots, :]).astype(jnp.bfloat16).astype(jnp.float32)
                    rows[(d * 3 + x) * 3 + c, :, lanes] = swap_tile(op)
    row = lax.broadcasted_iota(jnp.int32, (T, 256), 0)
    own = lax.broadcasted_iota(jnp.int32, (G, 256), 0) == (lax.broadcasted_iota(jnp.int32, (G, 256), 1) & (G - 1))

    def one_group(g, u):
        hot_u, ct_u = hot.at[u], ct.at[u]
        place = idx[pl.ds(g, 1), :]
        low = jnp.where(row == place % T, 1.0, 0.0).astype(jnp.bfloat16)
        part = jnp.broadcast_to(place // T, (8, 256))
        for t in range(WIN // T):
            chosen = jnp.where(part == t, 1.0, 0.0).astype(jnp.bfloat16)
            hot_u[t * T:(t + 1) * T, :] = low * jnp.concatenate([chosen] * (T // 8), axis=0)
        for p in range(27):
            ct_u[p * G:(p + 1) * G, :] = jnp.where(own, rows[p, pl.ds(g, 1), :], 0.0).astype(jnp.bfloat16)
        w = lax.dot_general(ct_u[...], hot_u[...], NT, preferred_element_type=jnp.float32).astype(jnp.bfloat16)
        for d in range(3):
            for x in range(3):
                for c in range(3):
                    p = (d * 3 + x) * 3 + c
                    out_ref[x, 0, pl.ds(pl.multiple_of(c * T + g * G, G), G), d * WIN:(d + 1) * WIN] = w[p * G:(p + 1) * G, :]

    def body(i, carry):
        for u in range(unroll):
            one_group(i * unroll + u, u)
        return carry

    lax.fori_loop(0, T // G // unroll, body, 0)


def make_operator(first, force, bond, nbr, counts, total_atoms, unroll=2):
    atoms = nbr.shape[1]
    blocks = atoms // T
    return pl.pallas_call(
        functools.partial(operator_kernel, total_atoms=total_atoms, unroll=unroll),
        grid_spec=pltpu.PrefetchScalarGridSpec(
            num_scalar_prefetch=1,
            grid=(blocks,),
            in_specs=[
                pl.BlockSpec((3, 3, 16, T), lambda s, f: (0, 0, 0, s)),
                pl.BlockSpec((3, 16, T), lambda s, f: (0, 0, s)),
                pl.BlockSpec((16, T), lambda s, f: (0, s)),
                pl.BlockSpec((1, T), lambda s, f: (0, s)),
            ],
            out_specs=pl.BlockSpec((3, 1, 3 * T, 3 * WIN), lambda s, f: (0, s, 0, 0)),
            scratch_shapes=[
                pltpu.VMEM((27, 8, 256), jnp.float32),
                pltpu.VMEM((8, 256), jnp.int32),
                pltpu.VMEM((unroll, WIN, 256), jnp.bfloat16),
                pltpu.VMEM((unroll, 27 * G, 256), jnp.bfloat16),
            ],
        ),
        out_shape=jax.ShapeDtypeStruct((3, blocks, 3 * T, 3 * WIN), jnp.bfloat16),
        cost_estimate=cost(2 * 27 * atoms * WIN * 256, 2 * 27 * atoms * WIN),
        name="operator",
    )(first, force, bond, nbr, counts)


def couple_kernel(core_ref, op_ref, left_ref, *refs, edges):
    step = pl.program_id(0)
    if edges:
        main_ref, low_ref, high_ref, sum_ref, keep_ref, send_ref, win, flux, acc = refs
    else:
        main_ref, acc, win, flux = refs
    shards, _, width, atoms = main_ref.shape
    cols = shards * width

    def fill(pieces):
        for m in range(shards):
            for d in range(3):
                at = d * WIN
                for ref, start, size in pieces:
                    win[m * width:(m + 1) * width, at:at + size] = ref[m, d, :, pl.ds(start, size)]
                    at += size

    for s in range(S // T):
        if edges:
            cut = REACH - s * T

            @pl.when(step == 0)
            def _():
                fill(((low_ref, s * T, cut), (main_ref, 0, WIN - cut)))

            @pl.when(step == 1)
            def _():
                over = (s + 1) * T
                fill(((main_ref, atoms - WIN + over, WIN - over), (high_ref, 0, over)))
        else:
            fill(((main_ref, pl.multiple_of(step * S + s * T, T), WIN),))
        block = op_ref[:, s].reshape(9 * T, 3 * WIN)
        f = lax.dot_general(block, win[...], NT, preferred_element_type=jnp.float32).astype(jnp.bfloat16)
        for x in range(3):
            for c in range(3):
                flux[c * S + s * T:c * S + (s + 1) * T, x * cols:(x + 1) * cols] = f[(x * 3 + c) * T:(x * 3 + c + 1) * T, :]
    part = jnp.dot(left_ref[0], flux[...], preferred_element_type=jnp.float32)
    if not edges:
        @pl.when(step == 0)
        def _():
            acc[...] = part

        @pl.when(step == 1)
        def _():
            acc[...] += part
    else:
        @pl.when(step == 0)
        def _():
            acc[...] = sum_ref[...] + part

        @pl.when(step == 1)
        def _():
            acc[...] += part
            mine = send_ref.shape[1]
            core = core_ref[0]
            for q in range(send_ref.shape[0]):
                keep_ref[q] = acc[pl.ds(pl.multiple_of((2 * q + core) * mine, 8), mine), :]
                send_ref[q] = acc[pl.ds(pl.multiple_of((2 * q + 1 - core) * mine, 8), mine), :]


def couple(core, operator, turned, main, low=None, high=None, so_far=None, chips=None):
    edges = low is not None
    shards, _, width, _ = main.shape
    cols = shards * width
    steps, modes, _ = turned.shape
    out = (modes, 3 * cols)
    at = (lambda b: b * (steps - 1)) if edges else (lambda b: b + 1)
    whole = lambda a: pl.BlockSpec(a.shape, lambda b, s: (0,) * a.ndim)
    scratch = [pltpu.VMEM((cols, 3 * WIN), jnp.bfloat16), pltpu.VMEM((3 * S, 3 * cols), jnp.bfloat16)]
    args = [operator, turned, main]
    if edges:
        half = (chips, modes // (2 * chips), 3 * cols)
        args += [low, high, so_far]
        out_shape = [jax.ShapeDtypeStruct(half, jnp.float32)] * 2
        out_specs = [pl.BlockSpec(half, lambda b, s: (0, 0, 0))] * 2
        scratch += [pltpu.VMEM(out, jnp.float32)]
    else:
        out_shape = jax.ShapeDtypeStruct(out, jnp.float32)
        out_specs = pl.BlockSpec(out, lambda b, s: (0, 0))
    return pl.pallas_call(
        functools.partial(couple_kernel, edges=edges),
        grid_spec=pltpu.PrefetchScalarGridSpec(
            num_scalar_prefetch=1,
            grid=(2,),
            in_specs=[
                pl.BlockSpec((3, S // T, 3 * T, 3 * WIN), lambda b, s: (0, at(b), 0, 0)),
                pl.BlockSpec((1, modes, 3 * S), lambda b, s: (at(b), 0, 0)),
            ]
            + [whole(a) for a in args[2:]],
            out_specs=out_specs,
            scratch_shapes=scratch,
        ),
        out_shape=out_shape,
        cost_estimate=cost(2 * 2 * S * 9 * cols * (3 * WIN + modes), 2 * 2 * S * 9 * 3 * WIN),
        name="edges" if edges else "middle",
    )(core, *args)


omega_step = 0.05
gamma = 0.1


def per_device(left_modes, right_panel, force_blocks, bond_vectors, neighbours, counts, left_bins, right_bins):
    atoms_dev = right_panel.shape[1]
    cols = right_panel.shape[2]
    modes_dev = left_modes.shape[2]
    n_modes = lax.axis_size("modes")
    n_atoms = lax.axis_size("atoms")
    total_atoms = atoms_dev * n_atoms
    me = lax.axis_index("atoms")
    n_core = 2
    n_chip = n_atoms // n_core
    mine = modes_dev // n_atoms

    shard = jnp.swapaxes(right_panel, 1, 2)
    main = lax.all_to_all(jnp.broadcast_to(shard[None], (n_modes,) + shard.shape), "modes", 0, 0, tiled=True)
    up = [(i, (i + 1) % n_atoms) for i in range(n_atoms)]
    down = [(i, (i - 1) % n_atoms) for i in range(n_atoms)]
    low = lax.ppermute(main[..., atoms_dev - REACH:], "atoms", up)
    high = lax.ppermute(main[..., :REACH], "atoms", down)

    first = (me * atoms_dev).astype(jnp.int32).reshape(1)
    core = (me % n_core).astype(jnp.int32).reshape(1)
    operator = make_operator(first, force_blocks, bond_vectors, neighbours, counts.reshape(1, -1), total_atoms, 4)
    turned = turn_left(left_modes)
    so_far = couple(core, operator, turned, main)
    keep, send = couple(core, operator, turned, main, low, high, so_far, n_chip)

    got = lax.ppermute(send, "atoms", [(i, i ^ 1) for i in range(n_atoms)])
    chip = (keep + got).astype(jnp.bfloat16)
    groups = [[c + n_core * i for i in range(n_chip)] for c in range(n_core)]
    parts = lax.all_to_all(chip, "atoms", 0, 0, axis_index_groups=groups, tiled=True)
    total = jnp.sum(parts.astype(jnp.float32), axis=0).reshape(mine, 3, -1)
    squares = jnp.sum(total * total, axis=1)

    omega_left = omega_step * left_bins.astype(jnp.float32)
    omega_right = omega_step * right_bins.astype(jnp.float32)
    freq_gap = omega_left[:, None] - omega_right[None, :]
    weight = gamma * gamma / (freq_gap * freq_gap + gamma * gamma)
    weight = weight * (omega_left[:, None] + omega_right[None, :]) ** 2 / (4.0 * omega_left[:, None] * omega_right[None, :])
    return 4.0 * jnp.sum(weight * squares, axis=1) / (total_atoms * n_modes * cols)


def solution(mesh):
    from jax.sharding import PartitionSpec as P

    return jax.shard_map(
        per_device,
        mesh=mesh,
        in_specs=(
            P(None, "atoms", "modes"),
            P(None, "atoms", "modes"),
            P(None, None, None, "atoms"),
            P(None, None, "atoms"),
            P(None, "atoms"),
            P("atoms"),
            P(("modes", "atoms")),
            P(),
        ),
        out_specs=P(("modes", "atoms")),
        check_vma=False,
    )
```

```python
import functools
import jax, jax.numpy as jnp
from jax import lax
from jax.experimental import pallas as pl
from jax.experimental.pallas import tpu as pltpu

REACH = 256
G = 16
T = 128
WIN = T + 2 * REACH
S = 2 * T
NT = (((1,), (1,)), ((), ()))


def in_vmem(a):
    return pltpu.with_memory_space_constraint(a, pltpu.VMEM)


def cost(flops, moved):
    return pl.CostEstimate(flops=flops, bytes_accessed=moved, transcendentals=0)


def swap_tile(t):
    row = lax.broadcasted_iota(jnp.int32, (8, 128), 0)
    col = lax.broadcasted_iota(jnp.int32, (8, 128), 1) // G
    for s in (4, 2, 1):
        low_row = (row & s) == 0
        same = (row & s) == (col & s)
        up = pltpu.roll(pltpu.roll(t, 8 - s, 0), G * s, 1)
        down = up if s == 4 else pltpu.roll(pltpu.roll(t, s, 0), 128 - G * s, 1)
        t = jnp.where(same, t, jnp.where(low_row, up, down))
    return t


def turn_kernel(left_ref, out_ref):
    unit = lax.broadcasted_iota(jnp.int32, (S, S), 0) == lax.broadcasted_iota(jnp.int32, (S, S), 1)
    unit = jnp.where(unit, 1.0, 0.0).astype(jnp.bfloat16)
    for c in range(3):
        for t in range(left_ref.shape[2] // S):
            cols = slice(t * S, (t + 1) * S)
            turned = lax.dot_general(unit, left_ref[c, :, cols], NT, preferred_element_type=jnp.float32)
            out_ref[0, cols, c * S:(c + 1) * S] = turned.astype(jnp.bfloat16)


def turn_left(left):
    _, atoms, modes = left.shape
    return pl.pallas_call(
        turn_kernel,
        grid=(atoms // S,),
        in_specs=[pl.BlockSpec((3, S, modes), lambda b: (0, b, 0))],
        out_specs=pl.BlockSpec((1, modes, 3 * S), lambda b: (b, 0, 0)),
        out_shape=jax.ShapeDtypeStruct((atoms // S, modes, 3 * S), jnp.bfloat16),
        compiler_params=pltpu.CompilerParams(vmem_limit_bytes=44 * 2**20),
        cost_estimate=cost(2 * left.size * S, 4 * left.size),
        name="turn",
    )(left)


def operator_kernel(first_ref, force_ref, bond_ref, nbr_ref, counts_ref, out_ref, rows, idx, hot, ct, *, total_atoms, unroll):
    step = pl.program_id(0)
    cnt = counts_ref[...]
    shift = first_ref[0] + step * T - REACH
    for h in range(2):
        lanes = slice(128 * h, 128 * h + 128)
        slots = slice(8 * h, 8 * h + 8)
        live = lax.broadcasted_iota(jnp.int32, (8, 128), 0) + 8 * h < cnt
        e = nbr_ref[slots, :] - shift
        e = jnp.where(e < 0, e + total_atoms, e)
        e = jnp.where(e >= total_atoms, e - total_atoms, e)
        idx[:, lanes] = swap_tile(e.astype(jnp.float32)).astype(jnp.int32)
        for x in range(3):
            scaled = jnp.where(live, bond_ref[x, slots, :], 0.0)
            for c in range(3):
                for d in range(3):
                    op = (scaled * force_ref[c, d, slots, :]).astype(jnp.bfloat16).astype(jnp.float32)
                    rows[(d * 3 + x) * 3 + c, :, lanes] = swap_tile(op)
    row = lax.broadcasted_iota(jnp.int32, (T, 256), 0)
    own = lax.broadcasted_iota(jnp.int32, (G, 256), 0) == (lax.broadcasted_iota(jnp.int32, (G, 256), 1) & (G - 1))

    def one_group(g, u):
        hot_u, ct_u = hot.at[u], ct.at[u]
        place = idx[pl.ds(g, 1), :]
        low = jnp.where(row == place % T, 1.0, 0.0).astype(jnp.bfloat16)
        part = jnp.broadcast_to(place // T, (8, 256))
        for t in range(WIN // T):
            chosen = jnp.where(part == t, 1.0, 0.0).astype(jnp.bfloat16)
            hot_u[t * T:(t + 1) * T, :] = low * jnp.concatenate([chosen] * (T // 8), axis=0)
        for p in range(27):
            ct_u[p * G:(p + 1) * G, :] = jnp.where(own, rows[p, pl.ds(g, 1), :], 0.0).astype(jnp.bfloat16)
        w = lax.dot_general(ct_u[...], hot_u[...], NT, preferred_element_type=jnp.float32).astype(jnp.bfloat16)
        for d in range(3):
            for x in range(3):
                for c in range(3):
                    p = (d * 3 + x) * 3 + c
                    out_ref[x, 0, pl.ds(pl.multiple_of(c * T + g * G, G), G), d * WIN:(d + 1) * WIN] = w[p * G:(p + 1) * G, :]

    def body(i, carry):
        for u in range(unroll):
            one_group(i * unroll + u, u)
        return carry

    lax.fori_loop(0, T // G // unroll, body, 0)


def make_operator(first, force, bond, nbr, counts, total_atoms, unroll=2):
    atoms = nbr.shape[1]
    blocks = atoms // T
    return pl.pallas_call(
        functools.partial(operator_kernel, total_atoms=total_atoms, unroll=unroll),
        grid_spec=pltpu.PrefetchScalarGridSpec(
            num_scalar_prefetch=1,
            grid=(blocks,),
            in_specs=[
                pl.BlockSpec((3, 3, 16, T), lambda s, f: (0, 0, 0, s)),
                pl.BlockSpec((3, 16, T), lambda s, f: (0, 0, s)),
                pl.BlockSpec((16, T), lambda s, f: (0, s)),
                pl.BlockSpec((1, T), lambda s, f: (0, s)),
            ],
            out_specs=pl.BlockSpec((3, 1, 3 * T, 3 * WIN), lambda s, f: (0, s, 0, 0)),
            scratch_shapes=[
                pltpu.VMEM((27, 8, 256), jnp.float32),
                pltpu.VMEM((8, 256), jnp.int32),
                pltpu.VMEM((unroll, WIN, 256), jnp.bfloat16),
                pltpu.VMEM((unroll, 27 * G, 256), jnp.bfloat16),
            ],
        ),
        out_shape=jax.ShapeDtypeStruct((3, blocks, 3 * T, 3 * WIN), jnp.bfloat16),
        compiler_params=pltpu.CompilerParams(vmem_limit_bytes=44 * 2**20),
        cost_estimate=cost(2 * 27 * atoms * WIN * 256, 2 * 27 * atoms * WIN),
        name="operator",
    )(first, force, bond, nbr, counts)


def fill(win, pieces):
    shards, _, width, _ = pieces[0][0].shape
    for m in range(shards):
        for d in range(3):
            at = d * WIN
            for ref, start, size in pieces:
                win[m * width:(m + 1) * width, at:at + size] = ref[m, d, :, pl.ds(start, size)]
                at += size


def flux_of(block, win):
    return lax.dot_general(block.reshape(9 * T, 3 * WIN), win[...], NT, preferred_element_type=jnp.float32).astype(jnp.bfloat16)


def middle_kernel(op_ref, main_ref, flux_ref, win):
    step = pl.program_id(0)
    cols = win.shape[0]
    fill(win, ((main_ref, pl.multiple_of(step * T, T), WIN),))
    f = flux_of(op_ref[:, 0], win)
    half = step // (S // T)
    at = pl.multiple_of(step % (S // T) * T, T)
    for x in range(3):
        for c in range(3):
            flux_ref[half, pl.ds(c * S + at, T), x * cols:(x + 1) * cols] = f[(x * 3 + c) * T:(x * 3 + c + 1) * T, :]


def middle(operator, main):
    shards, _, width, atoms = main.shape
    cols = shards * width
    inner = atoms - 2 * REACH
    return pl.pallas_call(
        middle_kernel,
        grid=(inner // T,),
        in_specs=[
            pl.BlockSpec((3, 1, 3 * T, 3 * WIN), lambda b: (0, b + REACH // T, 0, 0)),
            pl.BlockSpec(memory_space=pltpu.VMEM),
        ],
        out_specs=pl.BlockSpec(memory_space=pltpu.VMEM),
        out_shape=pltpu.VMEM((inner // S, 3 * S, 3 * cols), jnp.bfloat16),
        scratch_shapes=[pltpu.VMEM((cols, 3 * WIN), jnp.bfloat16)],
        compiler_params=pltpu.CompilerParams(vmem_limit_bytes=44 * 2**20),
        cost_estimate=cost(2 * inner * 9 * cols * 3 * WIN, 2 * inner * 9 * 3 * WIN),
        name="middle",
    )(operator, in_vmem(main))


def edges_kernel(core_ref, op_ref, left_ref, main_ref, low_ref, high_ref, mid_ref, keep_ref, send_ref, win, flux, acc):
    step = pl.program_id(0)
    atoms = main_ref.shape[3]
    cols = win.shape[0]
    ends = REACH // T
    for s in range(ends):
        @pl.when(step == s)
        def _():
            fill(win, ((low_ref, s * T, REACH - s * T), (main_ref, 0, WIN - REACH + s * T)))

        @pl.when(step == ends + s)
        def _():
            over = (s + 1) * T
            fill(win, ((main_ref, atoms - WIN + over, WIN - over), (high_ref, 0, over)))

    f = flux_of(op_ref[:, 0], win)
    at = pl.multiple_of(step % (S // T) * T, T)
    for x in range(3):
        for c in range(3):
            flux[pl.ds(c * S + at, T), x * cols:(x + 1) * cols] = f[(x * 3 + c) * T:(x * 3 + c + 1) * T, :]

    def add(left, fl):
        return jnp.dot(left, fl, preferred_element_type=jnp.float32)

    @pl.when(step == 0)
    def _():
        acc[...] = add(left_ref[0], mid_ref[0])

    @pl.when(step == 1)
    def _():
        acc[...] += add(left_ref[0], flux[...])

    @pl.when(step == 2)
    def _():
        acc[...] += add(left_ref[0], mid_ref[1])

    @pl.when(step == 3)
    def _():
        acc[...] += add(left_ref[0], flux[...])
        mine = send_ref.shape[1]
        core = core_ref[0]
        for q in range(send_ref.shape[0]):
            keep_ref[q] = acc[pl.ds(pl.multiple_of((2 * q + core) * mine, 8), mine), :]
            send_ref[q] = acc[pl.ds(pl.multiple_of((2 * q + 1 - core) * mine, 8), mine), :]


def edges(core, operator, turned, main, low, high, mid, chips):
    shards, _, width, atoms = main.shape
    cols = shards * width
    modes = turned.shape[1]
    ends = REACH // T
    half = (chips, modes // (2 * chips), 3 * cols)
    return pl.pallas_call(
        edges_kernel,
        grid_spec=pltpu.PrefetchScalarGridSpec(
            num_scalar_prefetch=1,
            grid=(2 * REACH // T,),
            in_specs=[
                pl.BlockSpec((3, 1, 3 * T, 3 * WIN), lambda b, s: (0, jnp.where(b < ends, b, b + atoms // T - 2 * ends), 0, 0)),
                pl.BlockSpec((1, modes, 3 * S), lambda b, s: (jnp.where(b < 2, 1 - b, b), 0, 0)),
            ]
            + [pl.BlockSpec(memory_space=pltpu.VMEM)] * 4,
            out_specs=[pl.BlockSpec(memory_space=pltpu.VMEM)] * 2,
            scratch_shapes=[
                pltpu.VMEM((cols, 3 * WIN), jnp.bfloat16),
                pltpu.VMEM((3 * S, 3 * cols), jnp.bfloat16),
                pltpu.VMEM((modes, 3 * cols), jnp.float32),
            ],
        ),
        out_shape=[pltpu.VMEM(half, jnp.float32)] * 2,
        compiler_params=pltpu.CompilerParams(vmem_limit_bytes=44 * 2**20),
        cost_estimate=cost(2 * 2 * REACH * 9 * cols * 3 * WIN + 2 * atoms * 9 * cols * modes, 2 * 2 * REACH * 9 * 3 * WIN),
        name="edges",
    )(core, operator, turned, *[in_vmem(a) for a in (main, low, high, mid)])


omega_step = 0.05
gamma = 0.1


def per_device(left_modes, right_panel, force_blocks, bond_vectors, neighbours, counts, left_bins, right_bins):
    atoms_dev = right_panel.shape[1]
    cols = right_panel.shape[2]
    modes_dev = left_modes.shape[2]
    n_modes = lax.axis_size("modes")
    n_atoms = lax.axis_size("atoms")
    total_atoms = atoms_dev * n_atoms
    me = lax.axis_index("atoms")
    n_core = 2
    n_chip = n_atoms // n_core
    mine = modes_dev // n_atoms

    shard = jnp.swapaxes(right_panel, 1, 2)
    main = lax.all_to_all(jnp.broadcast_to(shard[None], (n_modes,) + shard.shape), "modes", 0, 0, tiled=True)
    up = [(i, (i + 1) % n_atoms) for i in range(n_atoms)]
    down = [(i, (i - 1) % n_atoms) for i in range(n_atoms)]
    low = lax.ppermute(main[..., atoms_dev - REACH:], "atoms", up)
    high = lax.ppermute(main[..., :REACH], "atoms", down)

    first = (me * atoms_dev).astype(jnp.int32).reshape(1)
    core = (me % n_core).astype(jnp.int32).reshape(1)
    operator = make_operator(first, force_blocks, bond_vectors, neighbours, counts.reshape(1, -1), total_atoms, 4)
    turned = turn_left(left_modes)
    mid = middle(operator, main)
    keep, send = edges(core, operator, turned, main, low, high, mid, n_chip)

    got = lax.ppermute(send, "atoms", [(i, i ^ 1) for i in range(n_atoms)])
    chip = (keep + got).astype(jnp.bfloat16)
    groups = [[c + n_core * i for i in range(n_chip)] for c in range(n_core)]
    parts = lax.all_to_all(chip, "atoms", 0, 0, axis_index_groups=groups, tiled=True)
    total = jnp.sum(parts.astype(jnp.float32), axis=0).reshape(mine, 3, -1)
    squares = jnp.sum(total * total, axis=1)

    omega_left = omega_step * left_bins.astype(jnp.float32)
    omega_right = omega_step * right_bins.astype(jnp.float32)
    freq_gap = omega_left[:, None] - omega_right[None, :]
    weight = gamma * gamma / (freq_gap * freq_gap + gamma * gamma)
    weight = weight * (omega_left[:, None] + omega_right[None, :]) ** 2 / (4.0 * omega_left[:, None] * omega_right[None, :])
    return 4.0 * jnp.sum(weight * squares, axis=1) / (total_atoms * n_modes * cols)


def solution(mesh):
    from jax.sharding import PartitionSpec as P

    return jax.shard_map(
        per_device,
        mesh=mesh,
        in_specs=(
            P(None, "atoms", "modes"),
            P(None, "atoms", "modes"),
            P(None, None, None, "atoms"),
            P(None, None, "atoms"),
            P(None, "atoms"),
            P("atoms"),
            P(("modes", "atoms")),
            P(),
        ),
        out_specs=P(("modes", "atoms")),
        check_vma=False,
    )
```

```python
import functools
import jax, jax.numpy as jnp
from jax import lax
from jax.experimental import pallas as pl
from jax.experimental.pallas import tpu as pltpu

REACH = 256
G = 16
T = 128
WIN = T + 2 * REACH
S = 2 * T
NT = (((1,), (1,)), ((), ()))


def in_vmem(a):
    return pltpu.with_memory_space_constraint(a, pltpu.VMEM)


def cost(flops, moved):
    return pl.CostEstimate(flops=flops, bytes_accessed=moved, transcendentals=0)


def swap_tile(t):
    row = lax.broadcasted_iota(jnp.int32, (8, 128), 0)
    col = lax.broadcasted_iota(jnp.int32, (8, 128), 1) // G
    for s in (4, 2, 1):
        low_row = (row & s) == 0
        same = (row & s) == (col & s)
        up = pltpu.roll(pltpu.roll(t, 8 - s, 0), G * s, 1)
        down = up if s == 4 else pltpu.roll(pltpu.roll(t, s, 0), 128 - G * s, 1)
        t = jnp.where(same, t, jnp.where(low_row, up, down))
    return t


def operator_kernel(first_ref, force_ref, bond_ref, nbr_ref, counts_ref, left_ref, out_ref, turned_ref, rows, idx, hot, ct, *, total_atoms, unroll):
    step = pl.program_id(0)
    cnt = counts_ref[...]
    shift = first_ref[0] + step * T - REACH
    for h in range(2):
        lanes = slice(128 * h, 128 * h + 128)
        slots = slice(8 * h, 8 * h + 8)
        live = lax.broadcasted_iota(jnp.int32, (8, 128), 0) + 8 * h < cnt
        e = nbr_ref[slots, :] - shift
        e = jnp.where(e < 0, e + total_atoms, e)
        e = jnp.where(e >= total_atoms, e - total_atoms, e)
        idx[:, lanes] = swap_tile(e.astype(jnp.float32)).astype(jnp.int32)
        for x in range(3):
            scaled = jnp.where(live, bond_ref[x, slots, :], 0.0)
            for c in range(3):
                for d in range(3):
                    op = (scaled * force_ref[c, d, slots, :]).astype(jnp.bfloat16).astype(jnp.float32)
                    rows[(d * 3 + x) * 3 + c, :, lanes] = swap_tile(op)
    row = lax.broadcasted_iota(jnp.int32, (T, 256), 0)
    own = lax.broadcasted_iota(jnp.int32, (G, 256), 0) == (lax.broadcasted_iota(jnp.int32, (G, 256), 1) & (G - 1))

    def one_group(g, u):
        hot_u, ct_u = hot.at[u], ct.at[u]
        place = idx[pl.ds(g, 1), :]
        low = jnp.where(row == place % T, 1.0, 0.0).astype(jnp.bfloat16)
        part = jnp.broadcast_to(place // T, (8, 256))
        for t in range(WIN // T):
            chosen = jnp.where(part == t, 1.0, 0.0).astype(jnp.bfloat16)
            hot_u[t * T:(t + 1) * T, :] = low * jnp.concatenate([chosen] * (T // 8), axis=0)
        for p in range(27):
            ct_u[p * G:(p + 1) * G, :] = jnp.where(own, rows[p, pl.ds(g, 1), :], 0.0).astype(jnp.bfloat16)
        w = lax.dot_general(ct_u[...], hot_u[...], NT, preferred_element_type=jnp.float32).astype(jnp.bfloat16)
        for d in range(3):
            for x in range(3):
                for c in range(3):
                    p = (d * 3 + x) * 3 + c
                    out_ref[x, 0, pl.ds(pl.multiple_of(c * T + g * G, G), G), d * WIN:(d + 1) * WIN] = w[p * G:(p + 1) * G, :]

    rounds = T // G // unroll
    chunks = left_ref.shape[2] // T
    side = pl.multiple_of(step % (S // T) * T, T)

    def body(i, carry):
        for u in range(unroll):
            one_group(i * unroll + u, u)
            for q in range(u * 3 * chunks // rounds // unroll, (u + 1) * 3 * chunks // rounds // unroll):
                c, k = q % 3, q // 3
                cols = pl.ds(pl.multiple_of((i * (chunks // rounds) + k) * T, T), T)
                turned_ref[0, cols, pl.ds(c * S + side, T)] = left_ref[c, :, cols].T
        return carry

    lax.fori_loop(0, rounds, body, 0)


def make_operator(first, force, bond, nbr, counts, left, total_atoms, unroll=4):
    atoms = nbr.shape[1]
    modes = left.shape[2]
    blocks = atoms // T
    return pl.pallas_call(
        functools.partial(operator_kernel, total_atoms=total_atoms, unroll=unroll),
        grid_spec=pltpu.PrefetchScalarGridSpec(
            num_scalar_prefetch=1,
            grid=(blocks,),
            in_specs=[
                pl.BlockSpec((3, 3, 16, T), lambda s, f: (0, 0, 0, s)),
                pl.BlockSpec((3, 16, T), lambda s, f: (0, 0, s)),
                pl.BlockSpec((16, T), lambda s, f: (0, s)),
                pl.BlockSpec((1, T), lambda s, f: (0, s)),
                pl.BlockSpec((3, T, modes), lambda s, f: (0, s, 0)),
            ],
            out_specs=[
                pl.BlockSpec((3, 1, 3 * T, 3 * WIN), lambda s, f: (0, s, 0, 0)),
                pl.BlockSpec((1, modes, 3 * S), lambda s, f: (s // (S // T), 0, 0)),
            ],
            scratch_shapes=[
                pltpu.VMEM((27, 8, 256), jnp.float32),
                pltpu.VMEM((8, 256), jnp.int32),
                pltpu.VMEM((unroll, WIN, 256), jnp.bfloat16),
                pltpu.VMEM((unroll, 27 * G, 256), jnp.bfloat16),
            ],
        ),
        out_shape=[
            jax.ShapeDtypeStruct((3, blocks, 3 * T, 3 * WIN), jnp.bfloat16),
            jax.ShapeDtypeStruct((atoms // S, modes, 3 * S), jnp.bfloat16),
        ],
        compiler_params=pltpu.CompilerParams(vmem_limit_bytes=60 * 2**20),
        cost_estimate=cost(2 * 27 * atoms * WIN * 256, 2 * 27 * atoms * WIN),
        name="operator",
    )(first, force, bond, nbr, counts, left)


def fill(win, pieces):
    shards, _, width, _ = pieces[0][0].shape
    for m in range(shards):
        for d in range(3):
            at = d * WIN
            for ref, start, size in pieces:
                win[m * width:(m + 1) * width, at:at + size] = ref[m, d, :, pl.ds(start, size)]
                at += size


def flux_of(block, win):
    return lax.dot_general(block.reshape(9 * T, 3 * WIN), win[...], NT, preferred_element_type=jnp.float32).astype(jnp.bfloat16)


def middle_kernel(op_ref, main_ref, flux_ref, win):
    step = pl.program_id(0)
    cols = win.shape[0]
    fill(win, ((main_ref, pl.multiple_of(step * T, T), WIN),))
    f = flux_of(op_ref[:, 0], win)
    half = step // (S // T)
    at = pl.multiple_of(step % (S // T) * T, T)
    for x in range(3):
        for c in range(3):
            flux_ref[half, pl.ds(c * S + at, T), x * cols:(x + 1) * cols] = f[(x * 3 + c) * T:(x * 3 + c + 1) * T, :]


def middle(operator, main):
    shards, _, width, atoms = main.shape
    cols = shards * width
    inner = atoms - 2 * REACH
    return pl.pallas_call(
        middle_kernel,
        grid=(inner // T,),
        in_specs=[
            pl.BlockSpec((3, 1, 3 * T, 3 * WIN), lambda b: (0, b + REACH // T, 0, 0)),
            pl.BlockSpec(memory_space=pltpu.VMEM),
        ],
        out_specs=pl.BlockSpec(memory_space=pltpu.VMEM),
        out_shape=pltpu.VMEM((inner // S, 3 * S, 3 * cols), jnp.bfloat16),
        scratch_shapes=[pltpu.VMEM((cols, 3 * WIN), jnp.bfloat16)],
        compiler_params=pltpu.CompilerParams(vmem_limit_bytes=55 * 2**20),
        cost_estimate=cost(2 * inner * 9 * cols * 3 * WIN, 2 * inner * 9 * 3 * WIN),
        name="middle",
    )(operator, in_vmem(main))


def edges_kernel(core_ref, op_ref, left_ref, main_ref, low_ref, high_ref, mid_ref, keep_ref, send_ref, win, flux, acc):
    step = pl.program_id(0)
    atoms = main_ref.shape[3]
    cols = win.shape[0]
    ends = REACH // T
    for s in range(ends):
        @pl.when(step == s)
        def _():
            fill(win, ((low_ref, s * T, REACH - s * T), (main_ref, 0, WIN - REACH + s * T)))

        @pl.when(step == ends + s)
        def _():
            over = (s + 1) * T
            fill(win, ((main_ref, atoms - WIN + over, WIN - over), (high_ref, 0, over)))

    f = flux_of(op_ref[:, 0], win)
    at = pl.multiple_of(step % (S // T) * T, T)
    for x in range(3):
        for c in range(3):
            flux[pl.ds(c * S + at, T), x * cols:(x + 1) * cols] = f[(x * 3 + c) * T:(x * 3 + c + 1) * T, :]

    def add(left, fl):
        return jnp.dot(left, fl, preferred_element_type=jnp.float32)

    @pl.when(step == 0)
    def _():
        acc[...] = add(left_ref[0], mid_ref[0])

    @pl.when(step == 1)
    def _():
        acc[...] += add(left_ref[0], flux[...])

    @pl.when(step == 2)
    def _():
        acc[...] += add(left_ref[0], mid_ref[1])

    @pl.when(step == 3)
    def _():
        acc[...] += add(left_ref[0], flux[...])
        mine = send_ref.shape[1]
        core = core_ref[0]
        for q in range(send_ref.shape[0]):
            keep_ref[q] = acc[pl.ds(pl.multiple_of((2 * q + core) * mine, 8), mine), :]
            send_ref[q] = acc[pl.ds(pl.multiple_of((2 * q + 1 - core) * mine, 8), mine), :]


def edges(core, operator, turned, main, low, high, mid, chips):
    shards, _, width, atoms = main.shape
    cols = shards * width
    modes = turned.shape[1]
    ends = REACH // T
    half = (chips, modes // (2 * chips), 3 * cols)
    return pl.pallas_call(
        edges_kernel,
        grid_spec=pltpu.PrefetchScalarGridSpec(
            num_scalar_prefetch=1,
            grid=(2 * REACH // T,),
            in_specs=[
                pl.BlockSpec((3, 1, 3 * T, 3 * WIN), lambda b, s: (0, jnp.where(b < ends, b, b + atoms // T - 2 * ends), 0, 0)),
                pl.BlockSpec((1, modes, 3 * S), lambda b, s: (jnp.where(b < 2, 1 - b, b), 0, 0)),
            ]
            + [pl.BlockSpec(memory_space=pltpu.VMEM)] * 4,
            out_specs=[pl.BlockSpec(memory_space=pltpu.VMEM)] * 2,
            scratch_shapes=[
                pltpu.VMEM((cols, 3 * WIN), jnp.bfloat16),
                pltpu.VMEM((3 * S, 3 * cols), jnp.bfloat16),
                pltpu.VMEM((modes, 3 * cols), jnp.float32),
            ],
        ),
        out_shape=[pltpu.VMEM(half, jnp.float32)] * 2,
        compiler_params=pltpu.CompilerParams(vmem_limit_bytes=55 * 2**20),
        cost_estimate=cost(2 * 2 * REACH * 9 * cols * 3 * WIN + 2 * atoms * 9 * cols * modes, 2 * 2 * REACH * 9 * 3 * WIN),
        name="edges",
    )(core, operator, turned, *[in_vmem(a) for a in (main, low, high, mid)])


omega_step = 0.05
gamma = 0.1


def per_device(left_modes, right_panel, force_blocks, bond_vectors, neighbours, counts, left_bins, right_bins):
    atoms_dev = right_panel.shape[1]
    cols = right_panel.shape[2]
    modes_dev = left_modes.shape[2]
    n_modes = lax.axis_size("modes")
    n_atoms = lax.axis_size("atoms")
    total_atoms = atoms_dev * n_atoms
    me = lax.axis_index("atoms")
    n_core = 2
    n_chip = n_atoms // n_core
    mine = modes_dev // n_atoms

    shard = jnp.swapaxes(right_panel, 1, 2)
    main = lax.all_to_all(jnp.broadcast_to(shard[None], (n_modes,) + shard.shape), "modes", 0, 0, tiled=True)
    up = [(i, (i + 1) % n_atoms) for i in range(n_atoms)]
    down = [(i, (i - 1) % n_atoms) for i in range(n_atoms)]
    low = lax.ppermute(main[..., atoms_dev - REACH:], "atoms", up)
    high = lax.ppermute(main[..., :REACH], "atoms", down)

    first = (me * atoms_dev).astype(jnp.int32).reshape(1)
    core = (me % n_core).astype(jnp.int32).reshape(1)
    operator, turned = make_operator(first, force_blocks, bond_vectors, neighbours, counts.reshape(1, -1), left_modes, total_atoms)
    mid = middle(operator, main)
    keep, send = edges(core, operator, turned, main, low, high, mid, n_chip)

    got = lax.ppermute(send, "atoms", [(i, i ^ 1) for i in range(n_atoms)])
    chip = (keep + got).astype(jnp.bfloat16)
    groups = [[c + n_core * i for i in range(n_chip)] for c in range(n_core)]
    parts = lax.all_to_all(chip, "atoms", 0, 0, axis_index_groups=groups, tiled=True)
    total = jnp.sum(parts.astype(jnp.float32), axis=0).reshape(mine, 3, -1)
    squares = jnp.sum(total * total, axis=1)

    omega_left = omega_step * left_bins.astype(jnp.float32)
    omega_right = omega_step * right_bins.astype(jnp.float32)
    freq_gap = omega_left[:, None] - omega_right[None, :]
    weight = gamma * gamma / (freq_gap * freq_gap + gamma * gamma)
    weight = weight * (omega_left[:, None] + omega_right[None, :]) ** 2 / (4.0 * omega_left[:, None] * omega_right[None, :])
    return 4.0 * jnp.sum(weight * squares, axis=1) / (total_atoms * n_modes * cols)


def solution(mesh):
    from jax.sharding import PartitionSpec as P

    return jax.shard_map(
        per_device,
        mesh=mesh,
        in_specs=(
            P(None, "atoms", "modes"),
            P(None, "atoms", "modes"),
            P(None, None, None, "atoms"),
            P(None, None, "atoms"),
            P(None, "atoms"),
            P("atoms"),
            P(("modes", "atoms")),
            P(),
        ),
        out_specs=P(("modes", "atoms")),
        check_vma=False,
    )
```

```python
import functools
import jax, jax.numpy as jnp
from jax import lax
from jax.experimental import pallas as pl
from jax.experimental.pallas import tpu as pltpu

REACH = 256
G = 16
T = 128
WIN = T + 2 * REACH
S = 2 * T
NT = (((1,), (1,)), ((), ()))


def in_vmem(a):
    return pltpu.with_memory_space_constraint(a, pltpu.VMEM)


def cost(flops, moved):
    return pl.CostEstimate(flops=flops, bytes_accessed=moved, transcendentals=0)


def swap_tile(t):
    row = lax.broadcasted_iota(jnp.int32, (8, 128), 0)
    col = lax.broadcasted_iota(jnp.int32, (8, 128), 1) // G
    for s in (4, 2, 1):
        low_row = (row & s) == 0
        same = (row & s) == (col & s)
        up = pltpu.roll(pltpu.roll(t, 8 - s, 0), G * s, 1)
        down = up if s == 4 else pltpu.roll(pltpu.roll(t, s, 0), 128 - G * s, 1)
        t = jnp.where(same, t, jnp.where(low_row, up, down))
    return t


def spread_kernel(shard_ref, out_ref, sems):
    copies = [pltpu.make_async_copy(shard_ref, out_ref.at[m], sems.at[m]) for m in range(out_ref.shape[0])]
    for copy in copies:
        copy.start()
    for copy in copies:
        copy.wait()


def spread(shard, copies):
    return pl.pallas_call(
        spread_kernel,
        in_specs=[pl.BlockSpec(memory_space=pltpu.VMEM)],
        out_specs=pl.BlockSpec(memory_space=pl.ANY),
        out_shape=jax.ShapeDtypeStruct((copies,) + shard.shape, shard.dtype),
        scratch_shapes=[pltpu.SemaphoreType.DMA((copies,))],
        compiler_params=pltpu.CompilerParams(vmem_limit_bytes=63 * 2**20),
        name="spread",
    )(shard)


def operator_kernel(first_ref, force_ref, bond_ref, nbr_ref, counts_ref, left_ref, out_ref, turned_ref, rows, idx, hot, ct, *, total_atoms, unroll):
    step = pl.program_id(0)
    cnt = counts_ref[...]
    shift = first_ref[0] + step * T - REACH
    for h in range(2):
        lanes = slice(128 * h, 128 * h + 128)
        slots = slice(8 * h, 8 * h + 8)
        live = lax.broadcasted_iota(jnp.int32, (8, 128), 0) + 8 * h < cnt
        e = nbr_ref[slots, :] - shift
        e = jnp.where(e < 0, e + total_atoms, e)
        e = jnp.where(e >= total_atoms, e - total_atoms, e)
        idx[:, lanes] = swap_tile(e.astype(jnp.float32)).astype(jnp.int32)
        for x in range(3):
            scaled = jnp.where(live, bond_ref[x, slots, :], 0.0)
            for c in range(3):
                for d in range(3):
                    op = (scaled * force_ref[c, d, slots, :]).astype(jnp.bfloat16).astype(jnp.float32)
                    rows[(d * 3 + x) * 3 + c, :, lanes] = swap_tile(op)
    row = lax.broadcasted_iota(jnp.int32, (T, 256), 0)
    own = lax.broadcasted_iota(jnp.int32, (G, 256), 0) == (lax.broadcasted_iota(jnp.int32, (G, 256), 1) & (G - 1))

    def one_group(g, u):
        hot_u, ct_u = hot.at[u], ct.at[u]
        place = idx[pl.ds(g, 1), :]
        low = jnp.where(row == place % T, 1.0, 0.0).astype(jnp.bfloat16)
        part = jnp.broadcast_to(place // T, (8, 256))
        for t in range(WIN // T):
            chosen = jnp.where(part == t, 1.0, 0.0).astype(jnp.bfloat16)
            hot_u[t * T:(t + 1) * T, :] = low * jnp.concatenate([chosen] * (T // 8), axis=0)
        for p in range(27):
            ct_u[p * G:(p + 1) * G, :] = jnp.where(own, rows[p, pl.ds(g, 1), :], 0.0).astype(jnp.bfloat16)
        w = lax.dot_general(ct_u[...], hot_u[...], NT, preferred_element_type=jnp.float32).astype(jnp.bfloat16)
        for d in range(3):
            for x in range(3):
                for c in range(3):
                    p = (d * 3 + x) * 3 + c
                    out_ref[x, 0, pl.ds(pl.multiple_of(c * T + g * G, G), G), d * WIN:(d + 1) * WIN] = w[p * G:(p + 1) * G, :]

    rounds = T // G // unroll
    chunks = left_ref.shape[2] // T
    side = pl.multiple_of(step % (S // T) * T, T)

    def body(i, carry):
        for u in range(unroll):
            one_group(i * unroll + u, u)
            for q in range(u * 3 * chunks // rounds // unroll, (u + 1) * 3 * chunks // rounds // unroll):
                c, k = q % 3, q // 3
                cols = pl.ds(pl.multiple_of((i * (chunks // rounds) + k) * T, T), T)
                turned_ref[0, cols, pl.ds(c * S + side, T)] = left_ref[c, :, cols].T
        return carry

    lax.fori_loop(0, rounds, body, 0)


def make_operator(first, force, bond, nbr, counts, left, total_atoms, unroll=4):
    atoms = nbr.shape[1]
    modes = left.shape[2]
    blocks = atoms // T
    return pl.pallas_call(
        functools.partial(operator_kernel, total_atoms=total_atoms, unroll=unroll),
        grid_spec=pltpu.PrefetchScalarGridSpec(
            num_scalar_prefetch=1,
            grid=(blocks,),
            in_specs=[
                pl.BlockSpec((3, 3, 16, T), lambda s, f: (0, 0, 0, s)),
                pl.BlockSpec((3, 16, T), lambda s, f: (0, 0, s)),
                pl.BlockSpec((16, T), lambda s, f: (0, s)),
                pl.BlockSpec((1, T), lambda s, f: (0, s)),
                pl.BlockSpec((3, T, modes), lambda s, f: (0, s, 0)),
            ],
            out_specs=[
                pl.BlockSpec((3, 1, 3 * T, 3 * WIN), lambda s, f: (0, s, 0, 0)),
                pl.BlockSpec((1, modes, 3 * S), lambda s, f: (s // (S // T), 0, 0)),
            ],
            scratch_shapes=[
                pltpu.VMEM((27, 8, 256), jnp.float32),
                pltpu.VMEM((8, 256), jnp.int32),
                pltpu.VMEM((unroll, WIN, 256), jnp.bfloat16),
                pltpu.VMEM((unroll, 27 * G, 256), jnp.bfloat16),
            ],
        ),
        out_shape=[
            jax.ShapeDtypeStruct((3, blocks, 3 * T, 3 * WIN), jnp.bfloat16),
            jax.ShapeDtypeStruct((atoms // S, modes, 3 * S), jnp.bfloat16),
        ],
        compiler_params=pltpu.CompilerParams(vmem_limit_bytes=60 * 2**20),
        cost_estimate=cost(2 * 27 * atoms * WIN * 256, 2 * 27 * atoms * WIN),
        name="operator",
    )(first, force, bond, nbr, counts, left)


def fill(win, pieces):
    shards, _, width, _ = pieces[0][0].shape
    for m in range(shards):
        for d in range(3):
            at = d * WIN
            for ref, start, size in pieces:
                win[m * width:(m + 1) * width, at:at + size] = ref[m, d, :, pl.ds(start, size)]
                at += size


def flux_of(block, win):
    return lax.dot_general(block.reshape(9 * T, 3 * WIN), win[...], NT, preferred_element_type=jnp.float32).astype(jnp.bfloat16)


def keep_flux(flux, f, step):
    cols = f.shape[1]
    at = step % (S // T) * T
    for x in range(3):
        for c in range(3):
            flux[c * S + at:c * S + at + T, x * cols:(x + 1) * cols] = f[(x * 3 + c) * T:(x * 3 + c + 1) * T, :]


def middle_kernel(all_ref, main_ref, flux_ref, win, op, sems):
    step = pl.program_id(0)
    steps = op.shape[0]

    def fetch(e):
        return pltpu.make_async_copy(all_ref.at[:, e + REACH // T], op.at[e], sems.at[e])

    def one(e):
        if e == 0:
            for k in range(steps):
                fetch(k).start()
        fill(win, ((main_ref, e * T, WIN),))
        fetch(e).wait()
        keep_flux(flux_ref.at[e // (S // T)], flux_of(op[e], win), e)

    for e in range(steps):
        @pl.when(step == e)
        def _():
            one(e)


def middle(operator, main):
    shards, _, width, atoms = main.shape
    cols = shards * width
    inner = atoms - 2 * REACH
    return pl.pallas_call(
        middle_kernel,
        grid=(inner // T,),
        in_specs=[pl.BlockSpec(memory_space=pl.ANY), pl.BlockSpec(memory_space=pltpu.VMEM)],
        out_specs=pl.BlockSpec(memory_space=pltpu.VMEM),
        out_shape=pltpu.VMEM((inner // S, 3 * S, 3 * cols), jnp.bfloat16),
        scratch_shapes=[
            pltpu.VMEM((cols, 3 * WIN), jnp.bfloat16),
            pltpu.VMEM((inner // T, 3, 3 * T, 3 * WIN), jnp.bfloat16),
            pltpu.SemaphoreType.DMA((inner // T,)),
        ],
        compiler_params=pltpu.CompilerParams(vmem_limit_bytes=55 * 2**20),
        cost_estimate=cost(2 * inner * 9 * cols * 3 * WIN, 2 * inner * 9 * 3 * WIN),
        name="middle",
    )(operator, in_vmem(main))


def edges_kernel(core_ref, all_ref, left_ref, main_ref, low_ref, high_ref, mid_ref, keep_ref, send_ref, win, flux, acc, op, sems):
    step = pl.program_id(0)
    atoms = main_ref.shape[3]
    ends = REACH // T
    blocks = atoms // T
    slots = op.shape[0]

    def fetch(e):
        block = e if e < ends else e + blocks - 2 * ends
        return pltpu.make_async_copy(all_ref.at[:, block], op.at[e % slots], sems.at[e % slots])

    def add(fl):
        return jnp.dot(left_ref[0], fl, preferred_element_type=jnp.float32)

    def one(e):
        if e + 2 < 2 * ends:
            fetch(e + 2).start()
        if e < ends:
            fill(win, ((low_ref, e * T, REACH - e * T), (main_ref, 0, WIN - REACH + e * T)))
        else:
            over = (e - ends + 1) * T
            fill(win, ((main_ref, atoms - WIN + over, WIN - over), (high_ref, 0, over)))
        fetch(e).wait()
        keep_flux(flux, flux_of(op[e % slots], win), e)

    @pl.when(step == 0)
    def _():
        fetch(0).start()
        acc[...] = add(mid_ref[0])

    @pl.when(step == 1)
    def _():
        fetch(1).start()
        acc[...] += add(mid_ref[1])

    for e in range(2 * ends):
        @pl.when(step == e + 2)
        def _():
            one(e)

    @pl.when(step == 3)
    def _():
        acc[...] += add(flux[...])

    @pl.when(step == 5)
    def _():
        acc[...] += add(flux[...])
        mine = send_ref.shape[1]
        core = core_ref[0]
        for q in range(send_ref.shape[0]):
            keep_ref[q] = acc[pl.ds(pl.multiple_of((2 * q + core) * mine, 8), mine), :]
            send_ref[q] = acc[pl.ds(pl.multiple_of((2 * q + 1 - core) * mine, 8), mine), :]


def edges(core, operator, turned, main, low, high, mid, chips):
    shards, _, width, atoms = main.shape
    cols = shards * width
    steps, modes, _ = turned.shape
    ends = REACH // T
    slots = 2 * ends - 1
    half = (chips, modes // (2 * chips), 3 * cols)
    part = lambda b: jnp.where(b < 2, b + 1, jnp.where(b < 4, 0, steps - 1))
    return pl.pallas_call(
        edges_kernel,
        grid_spec=pltpu.PrefetchScalarGridSpec(
            num_scalar_prefetch=1,
            grid=(2 + 2 * ends,),
            in_specs=[
                pl.BlockSpec(memory_space=pl.ANY),
                pl.BlockSpec((1, modes, 3 * S), lambda b, s: (part(b), 0, 0)),
            ]
            + [pl.BlockSpec(memory_space=pltpu.VMEM)] * 4,
            out_specs=[pl.BlockSpec(memory_space=pltpu.VMEM)] * 2,
            scratch_shapes=[
                pltpu.VMEM((cols, 3 * WIN), jnp.bfloat16),
                pltpu.VMEM((3 * S, 3 * cols), jnp.bfloat16),
                pltpu.VMEM((modes, 3 * cols), jnp.float32),
                pltpu.VMEM((slots, 3, 3 * T, 3 * WIN), jnp.bfloat16),
                pltpu.SemaphoreType.DMA((slots,)),
            ],
        ),
        out_shape=[pltpu.VMEM(half, jnp.float32)] * 2,
        compiler_params=pltpu.CompilerParams(vmem_limit_bytes=55 * 2**20),
        cost_estimate=cost(2 * 2 * REACH * 9 * cols * 3 * WIN + 2 * atoms * 9 * cols * modes, 2 * 2 * REACH * 9 * 3 * WIN),
        name="edges",
    )(core, operator, turned, *[in_vmem(a) for a in (main, low, high, mid)])


omega_step = 0.05
gamma = 0.1


def per_device(left_modes, right_panel, force_blocks, bond_vectors, neighbours, counts, left_bins, right_bins):
    atoms_dev = right_panel.shape[1]
    cols = right_panel.shape[2]
    modes_dev = left_modes.shape[2]
    n_modes = lax.axis_size("modes")
    n_atoms = lax.axis_size("atoms")
    total_atoms = atoms_dev * n_atoms
    me = lax.axis_index("atoms")
    n_core = 2
    n_chip = n_atoms // n_core
    mine = modes_dev // n_atoms

    shard = jnp.swapaxes(right_panel, 1, 2)
    main = lax.all_to_all(spread(shard, n_modes), "modes", 0, 0, tiled=True)
    up = [(i, (i + 1) % n_atoms) for i in range(n_atoms)]
    down = [(i, (i - 1) % n_atoms) for i in range(n_atoms)]
    low = lax.ppermute(main[..., atoms_dev - REACH:], "atoms", up)
    high = lax.ppermute(main[..., :REACH], "atoms", down)

    first = (me * atoms_dev).astype(jnp.int32).reshape(1)
    core = (me % n_core).astype(jnp.int32).reshape(1)
    operator, turned = make_operator(first, force_blocks, bond_vectors, neighbours, counts.reshape(1, -1), left_modes, total_atoms, 8)
    mid = middle(operator, main)
    keep, send = edges(core, operator, turned, main, low, high, mid, n_chip)

    omega_left = omega_step * left_bins.astype(jnp.float32)
    omega_right = omega_step * right_bins.astype(jnp.float32)
    freq_gap = omega_left[:, None] - omega_right[None, :]
    weight = gamma * gamma / (freq_gap * freq_gap + gamma * gamma)
    weight = weight * (omega_left[:, None] + omega_right[None, :]) ** 2 / (4.0 * omega_left[:, None] * omega_right[None, :])
    weight = weight * (4.0 / (total_atoms * n_modes * cols))

    got = lax.ppermute(send, "atoms", [(i, i ^ 1) for i in range(n_atoms)])
    chip = (keep + got).astype(jnp.bfloat16)
    groups = [[c + n_core * i for i in range(n_chip)] for c in range(n_core)]
    parts = lax.all_to_all(chip, "atoms", 0, 0, axis_index_groups=groups, tiled=True)
    width = weight.shape[1]
    total = jnp.sum(parts.astype(jnp.float32), axis=0)
    squares = sum(total[:, x * width:(x + 1) * width] ** 2 for x in range(3))
    return jnp.sum(weight * squares, axis=1)


def solution(mesh):
    from jax.sharding import PartitionSpec as P

    return jax.shard_map(
        per_device,
        mesh=mesh,
        in_specs=(
            P(None, "atoms", "modes"),
            P(None, "atoms", "modes"),
            P(None, None, None, "atoms"),
            P(None, None, "atoms"),
            P(None, "atoms"),
            P("atoms"),
            P(("modes", "atoms")),
            P(),
        ),
        out_specs=P(("modes", "atoms")),
        check_vma=False,
    )
```

```python
import functools
import jax, jax.numpy as jnp
from jax import lax
from jax.experimental import pallas as pl
from jax.experimental.pallas import tpu as pltpu

REACH = 256
G = 16
T = 128
WIN = T + 2 * REACH
S = 2 * T
NT = (((1,), (1,)), ((), ()))
TN = (((0,), (0,)), ((), ()))


def in_vmem(a):
    return pltpu.with_memory_space_constraint(a, pltpu.VMEM)


def cost(flops, moved):
    return pl.CostEstimate(flops=flops, bytes_accessed=moved, transcendentals=0)


def swap_tile(t):
    row = lax.broadcasted_iota(jnp.int32, (8, 128), 0)
    col = lax.broadcasted_iota(jnp.int32, (8, 128), 1) // G
    for s in (4, 2, 1):
        low_row = (row & s) == 0
        same = (row & s) == (col & s)
        up = pltpu.roll(pltpu.roll(t, 8 - s, 0), G * s, 1)
        down = up if s == 4 else pltpu.roll(pltpu.roll(t, s, 0), 128 - G * s, 1)
        t = jnp.where(same, t, jnp.where(low_row, up, down))
    return t


def spread_kernel(shard_ref, out_ref, sems):
    copies = [pltpu.make_async_copy(shard_ref, out_ref.at[m], sems.at[m]) for m in range(out_ref.shape[0])]
    for copy in copies:
        copy.start()
    for copy in copies:
        copy.wait()


def spread(shard, copies):
    return pl.pallas_call(
        spread_kernel,
        in_specs=[pl.BlockSpec(memory_space=pltpu.VMEM)],
        out_specs=pl.BlockSpec(memory_space=pl.ANY),
        out_shape=jax.ShapeDtypeStruct((copies,) + shard.shape, shard.dtype),
        scratch_shapes=[pltpu.SemaphoreType.DMA((copies,))],
        compiler_params=pltpu.CompilerParams(vmem_limit_bytes=63 * 2**20),
        name="spread",
    )(shard)


def operator_kernel(first_ref, force_ref, bond_ref, nbr_ref, counts_ref, out_ref, rows, idx, hot, ct, *, total_atoms, unroll):
    step = pl.program_id(0)
    cnt = counts_ref[...]
    shift = first_ref[0] + step * T - REACH
    for h in range(2):
        lanes = slice(128 * h, 128 * h + 128)
        slots = slice(8 * h, 8 * h + 8)
        live = lax.broadcasted_iota(jnp.int32, (8, 128), 0) + 8 * h < cnt
        e = nbr_ref[slots, :] - shift
        e = jnp.where(e < 0, e + total_atoms, e)
        e = jnp.where(e >= total_atoms, e - total_atoms, e)
        idx[:, lanes] = swap_tile(e.astype(jnp.float32)).astype(jnp.int32)
        for x in range(3):
            scaled = jnp.where(live, bond_ref[x, slots, :], 0.0)
            for c in range(3):
                for d in range(3):
                    op = (scaled * force_ref[c, d, slots, :]).astype(jnp.bfloat16).astype(jnp.float32)
                    rows[(d * 3 + x) * 3 + c, :, lanes] = swap_tile(op)
    row = lax.broadcasted_iota(jnp.int32, (T, 256), 0)
    own = lax.broadcasted_iota(jnp.int32, (G, 256), 0) == (lax.broadcasted_iota(jnp.int32, (G, 256), 1) & (G - 1))

    def one_group(g, u):
        hot_u, ct_u = hot.at[u], ct.at[u]
        place = idx[pl.ds(g, 1), :]
        low = jnp.where(row == place % T, 1.0, 0.0).astype(jnp.bfloat16)
        part = jnp.broadcast_to(place // T, (8, 256))
        for t in range(WIN // T):
            chosen = jnp.where(part == t, 1.0, 0.0).astype(jnp.bfloat16)
            hot_u[t * T:(t + 1) * T, :] = low * jnp.concatenate([chosen] * (T // 8), axis=0)
        for p in range(27):
            ct_u[p * G:(p + 1) * G, :] = jnp.where(own, rows[p, pl.ds(g, 1), :], 0.0).astype(jnp.bfloat16)
        w = lax.dot_general(ct_u[...], hot_u[...], NT, preferred_element_type=jnp.float32).astype(jnp.bfloat16)
        for d in range(3):
            for x in range(3):
                for c in range(3):
                    p = (d * 3 + x) * 3 + c
                    out_ref[x, 0, pl.ds(pl.multiple_of(c * T + g * G, G), G), d * WIN:(d + 1) * WIN] = w[p * G:(p + 1) * G, :]

    rounds = T // G // unroll

    def body(i, carry):
        for u in range(unroll):
            one_group(i * unroll + u, u)
        return carry

    lax.fori_loop(0, rounds, body, 0)


def make_operator(first, force, bond, nbr, counts, total_atoms, unroll=4):
    atoms = nbr.shape[1]
    blocks = atoms // T
    return pl.pallas_call(
        functools.partial(operator_kernel, total_atoms=total_atoms, unroll=unroll),
        grid_spec=pltpu.PrefetchScalarGridSpec(
            num_scalar_prefetch=1,
            grid=(blocks,),
            in_specs=[
                pl.BlockSpec((3, 3, 16, T), lambda s, f: (0, 0, 0, s)),
                pl.BlockSpec((3, 16, T), lambda s, f: (0, 0, s)),
                pl.BlockSpec((16, T), lambda s, f: (0, s)),
                pl.BlockSpec((1, T), lambda s, f: (0, s)),
            ],
            out_specs=pl.BlockSpec((3, 1, 3 * T, 3 * WIN), lambda s, f: (0, s, 0, 0)),
            scratch_shapes=[
                pltpu.VMEM((27, 8, 256), jnp.float32),
                pltpu.VMEM((8, 256), jnp.int32),
                pltpu.VMEM((unroll, WIN, 256), jnp.bfloat16),
                pltpu.VMEM((unroll, 27 * G, 256), jnp.bfloat16),
            ],
        ),
        out_shape=jax.ShapeDtypeStruct((3, blocks, 3 * T, 3 * WIN), jnp.bfloat16),
        compiler_params=pltpu.CompilerParams(vmem_limit_bytes=60 * 2**20),
        cost_estimate=cost(2 * 27 * atoms * WIN * 256, 2 * 27 * atoms * WIN),
        name="operator",
    )(first, force, bond, nbr, counts)


def fill(win, pieces):
    shards, _, width, _ = pieces[0][0].shape
    for m in range(shards):
        for d in range(3):
            at = d * WIN
            for ref, start, size in pieces:
                win[m * width:(m + 1) * width, at:at + size] = ref[m, d, :, pl.ds(start, size)]
                at += size


def flux_of(block, win):
    return lax.dot_general(block.reshape(9 * T, 3 * WIN), win[...], NT, preferred_element_type=jnp.float32).astype(jnp.bfloat16)


def keep_flux(flux, f, step):
    cols = f.shape[1]
    at = step % (S // T) * T
    for x in range(3):
        for c in range(3):
            flux[c * S + at:c * S + at + T, x * cols:(x + 1) * cols] = f[(x * 3 + c) * T:(x * 3 + c + 1) * T, :]


def middle_kernel(all_ref, main_ref, flux_ref, win, op, sems):
    step = pl.program_id(0)
    steps = op.shape[0]

    def fetch(e):
        return pltpu.make_async_copy(all_ref.at[:, e + REACH // T], op.at[e], sems.at[e])

    def one(e):
        if e == 0:
            for k in range(steps):
                fetch(k).start()
        fill(win, ((main_ref, e * T, WIN),))
        fetch(e).wait()
        keep_flux(flux_ref.at[e // (S // T)], flux_of(op[e], win), e)

    for e in range(steps):
        @pl.when(step == e)
        def _():
            one(e)


def middle(operator, main):
    shards, _, width, atoms = main.shape
    cols = shards * width
    inner = atoms - 2 * REACH
    return pl.pallas_call(
        middle_kernel,
        grid=(inner // T,),
        in_specs=[pl.BlockSpec(memory_space=pl.ANY), pl.BlockSpec(memory_space=pltpu.VMEM)],
        out_specs=pl.BlockSpec(memory_space=pltpu.VMEM),
        out_shape=pltpu.VMEM((inner // S, 3 * S, 3 * cols), jnp.bfloat16),
        scratch_shapes=[
            pltpu.VMEM((cols, 3 * WIN), jnp.bfloat16),
            pltpu.VMEM((inner // T, 3, 3 * T, 3 * WIN), jnp.bfloat16),
            pltpu.SemaphoreType.DMA((inner // T,)),
        ],
        compiler_params=pltpu.CompilerParams(vmem_limit_bytes=55 * 2**20),
        cost_estimate=cost(2 * inner * 9 * cols * 3 * WIN, 2 * inner * 9 * 3 * WIN),
        name="middle",
    )(operator, in_vmem(main))


def edges_kernel(core_ref, all_ref, left_ref, main_ref, low_ref, high_ref, mid_ref, keep_ref, send_ref, win, flux, acc, op, sems):
    step = pl.program_id(0)
    atoms = main_ref.shape[3]
    ends = REACH // T
    blocks = atoms // T
    slots = op.shape[0]

    def fetch(e):
        block = e if e < ends else e + blocks - 2 * ends
        return pltpu.make_async_copy(all_ref.at[:, block], op.at[e % slots], sems.at[e % slots])

    def add(fl):
        left = left_ref[...].reshape(3 * S, left_ref.shape[2])
        return lax.dot_general(left, fl, TN, preferred_element_type=jnp.float32)

    def one(e):
        if e + 2 < 2 * ends:
            fetch(e + 2).start()
        if e < ends:
            fill(win, ((low_ref, e * T, REACH - e * T), (main_ref, 0, WIN - REACH + e * T)))
        else:
            over = (e - ends + 1) * T
            fill(win, ((main_ref, atoms - WIN + over, WIN - over), (high_ref, 0, over)))
        fetch(e).wait()
        keep_flux(flux, flux_of(op[e % slots], win), e)

    @pl.when(step == 0)
    def _():
        fetch(0).start()
        acc[...] = add(mid_ref[0])

    @pl.when(step == 1)
    def _():
        fetch(1).start()
        acc[...] += add(mid_ref[1])

    for e in range(2 * ends):
        @pl.when(step == e + 2)
        def _():
            one(e)

    @pl.when(step == 3)
    def _():
        acc[...] += add(flux[...])

    @pl.when(step == 5)
    def _():
        acc[...] += add(flux[...])
        mine = send_ref.shape[1]
        core = core_ref[0]
        for q in range(send_ref.shape[0]):
            keep_ref[q] = acc[pl.ds(pl.multiple_of((2 * q + core) * mine, 8), mine), :]
            send_ref[q] = acc[pl.ds(pl.multiple_of((2 * q + 1 - core) * mine, 8), mine), :]


def edges(core, operator, left, main, low, high, mid, chips):
    shards, _, width, atoms = main.shape
    cols = shards * width
    steps, modes = atoms // S, left.shape[2]
    ends = REACH // T
    slots = 2 * ends - 1
    half = (chips, modes // (2 * chips), 3 * cols)
    part = lambda b: jnp.where(b < 2, b + 1, jnp.where(b < 4, 0, steps - 1))
    return pl.pallas_call(
        edges_kernel,
        grid_spec=pltpu.PrefetchScalarGridSpec(
            num_scalar_prefetch=1,
            grid=(2 + 2 * ends,),
            in_specs=[
                pl.BlockSpec(memory_space=pl.ANY),
                pl.BlockSpec((3, S, modes), lambda b, s: (0, part(b), 0)),
            ]
            + [pl.BlockSpec(memory_space=pltpu.VMEM)] * 4,
            out_specs=[pl.BlockSpec(memory_space=pltpu.VMEM)] * 2,
            scratch_shapes=[
                pltpu.VMEM((cols, 3 * WIN), jnp.bfloat16),
                pltpu.VMEM((3 * S, 3 * cols), jnp.bfloat16),
                pltpu.VMEM((modes, 3 * cols), jnp.float32),
                pltpu.VMEM((slots, 3, 3 * T, 3 * WIN), jnp.bfloat16),
                pltpu.SemaphoreType.DMA((slots,)),
            ],
        ),
        out_shape=[pltpu.VMEM(half, jnp.float32)] * 2,
        compiler_params=pltpu.CompilerParams(vmem_limit_bytes=55 * 2**20),
        cost_estimate=cost(2 * 2 * REACH * 9 * cols * 3 * WIN + 2 * atoms * 9 * cols * modes, 2 * 2 * REACH * 9 * 3 * WIN),
        name="edges",
    )(core, operator, left, *[in_vmem(a) for a in (main, low, high, mid)])


omega_step = 0.05
gamma = 0.1


def per_device(left_modes, right_panel, force_blocks, bond_vectors, neighbours, counts, left_bins, right_bins):
    atoms_dev = right_panel.shape[1]
    cols = right_panel.shape[2]
    modes_dev = left_modes.shape[2]
    n_modes = lax.axis_size("modes")
    n_atoms = lax.axis_size("atoms")
    total_atoms = atoms_dev * n_atoms
    me = lax.axis_index("atoms")
    n_core = 2
    n_chip = n_atoms // n_core
    mine = modes_dev // n_atoms

    shard = jnp.swapaxes(right_panel, 1, 2)
    main = lax.all_to_all(spread(shard, n_modes), "modes", 0, 0, tiled=True)
    up = [(i, (i + 1) % n_atoms) for i in range(n_atoms)]
    down = [(i, (i - 1) % n_atoms) for i in range(n_atoms)]
    low = lax.ppermute(main[..., atoms_dev - REACH:], "atoms", up)
    high = lax.ppermute(main[..., :REACH], "atoms", down)

    first = (me * atoms_dev).astype(jnp.int32).reshape(1)
    core = (me % n_core).astype(jnp.int32).reshape(1)
    operator = make_operator(first, force_blocks, bond_vectors, neighbours, counts.reshape(1, -1), total_atoms, 8)
    mid = middle(operator, main)
    keep, send = edges(core, operator, left_modes, main, low, high, mid, n_chip)

    omega_left = omega_step * left_bins.astype(jnp.float32)
    omega_right = omega_step * right_bins.astype(jnp.float32)
    freq_gap = omega_left[:, None] - omega_right[None, :]
    weight = gamma * gamma / (freq_gap * freq_gap + gamma * gamma)
    weight = weight * (omega_left[:, None] + omega_right[None, :]) ** 2 / (4.0 * omega_left[:, None] * omega_right[None, :])
    weight = weight * (4.0 / (total_atoms * n_modes * cols))

    got = lax.ppermute(send, "atoms", [(i, i ^ 1) for i in range(n_atoms)])
    chip = (keep + got).astype(jnp.bfloat16)
    groups = [[c + n_core * i for i in range(n_chip)] for c in range(n_core)]
    parts = lax.all_to_all(chip, "atoms", 0, 0, axis_index_groups=groups, tiled=True)
    width = weight.shape[1]
    total = jnp.sum(parts.astype(jnp.float32), axis=0)
    squares = sum(total[:, x * width:(x + 1) * width] ** 2 for x in range(3))
    return jnp.sum(weight * squares, axis=1)


def solution(mesh):
    from jax.sharding import PartitionSpec as P

    return jax.shard_map(
        per_device,
        mesh=mesh,
        in_specs=(
            P(None, "atoms", "modes"),
            P(None, "atoms", "modes"),
            P(None, None, None, "atoms"),
            P(None, None, "atoms"),
            P(None, "atoms"),
            P("atoms"),
            P(("modes", "atoms")),
            P(),
        ),
        out_specs=P(("modes", "atoms")),
        check_vma=False,
    )
```

```python
import functools
import jax, jax.numpy as jnp
from jax import lax
from jax.experimental import pallas as pl
from jax.experimental.pallas import tpu as pltpu

REACH = 256
G = 16
T = 128
WIN = T + 2 * REACH
S = 2 * T
NT = (((1,), (1,)), ((), ()))
TN = (((0,), (0,)), ((), ()))


def in_vmem(a):
    return pltpu.with_memory_space_constraint(a, pltpu.VMEM)


def cost(flops, moved):
    return pl.CostEstimate(flops=flops, bytes_accessed=moved, transcendentals=0)


def swap_tile(t):
    row = lax.broadcasted_iota(jnp.int32, (8, 128), 0)
    col = lax.broadcasted_iota(jnp.int32, (8, 128), 1) // G
    for s in (4, 2, 1):
        low_row = (row & s) == 0
        same = (row & s) == (col & s)
        up = pltpu.roll(pltpu.roll(t, 8 - s, 0), G * s, 1)
        down = up if s == 4 else pltpu.roll(pltpu.roll(t, s, 0), 128 - G * s, 1)
        t = jnp.where(same, t, jnp.where(low_row, up, down))
    return t


def spread_kernel(shard_ref, out_ref, sems):
    copies = [pltpu.make_async_copy(shard_ref, out_ref.at[m], sems.at[m]) for m in range(out_ref.shape[0])]
    for copy in copies:
        copy.start()
    for copy in copies:
        copy.wait()


def spread(shard, copies):
    return pl.pallas_call(
        spread_kernel,
        in_specs=[pl.BlockSpec(memory_space=pltpu.VMEM)],
        out_specs=pl.BlockSpec(memory_space=pl.ANY),
        out_shape=jax.ShapeDtypeStruct((copies,) + shard.shape, shard.dtype),
        scratch_shapes=[pltpu.SemaphoreType.DMA((copies,))],
        compiler_params=pltpu.CompilerParams(vmem_limit_bytes=63 * 2**20),
        name="spread",
    )(shard)


def operator_kernel(first_ref, force_ref, bond_ref, nbr_ref, counts_ref, out_ref, rows, idx, hot, ct, *, total_atoms, unroll):
    step = pl.program_id(0)
    cnt = counts_ref[...]
    shift = first_ref[0] + step * T - REACH
    for h in range(2):
        lanes = slice(128 * h, 128 * h + 128)
        slots = slice(8 * h, 8 * h + 8)
        live = lax.broadcasted_iota(jnp.int32, (8, 128), 0) + 8 * h < cnt
        e = nbr_ref[slots, :] - shift
        e = jnp.where(e < 0, e + total_atoms, e)
        e = jnp.where(e >= total_atoms, e - total_atoms, e)
        idx[:, lanes] = swap_tile(e.astype(jnp.float32)).astype(jnp.int32)
        for x in range(3):
            scaled = jnp.where(live, bond_ref[x, slots, :], 0.0)
            for c in range(3):
                for d in range(3):
                    op = (scaled * force_ref[c, d, slots, :]).astype(jnp.bfloat16).astype(jnp.float32)
                    rows[(d * 3 + x) * 3 + c, :, lanes] = swap_tile(op)
    row = lax.broadcasted_iota(jnp.int32, (T, 256), 0)
    own = lax.broadcasted_iota(jnp.int32, (G, 256), 0) == (lax.broadcasted_iota(jnp.int32, (G, 256), 1) & (G - 1))

    def one_group(g, u):
        hot_u, ct_u = hot.at[u], ct.at[u]
        place = idx[pl.ds(g, 1), :]
        low = jnp.where(row == place % T, 1.0, 0.0).astype(jnp.bfloat16)
        part = jnp.broadcast_to(place // T, (8, 256))
        for t in range(WIN // T):
            chosen = jnp.where(part == t, 1.0, 0.0).astype(jnp.bfloat16)
            hot_u[t * T:(t + 1) * T, :] = low * jnp.concatenate([chosen] * (T // 8), axis=0)
        for p in range(27):
            ct_u[p * G:(p + 1) * G, :] = jnp.where(own, rows[p, pl.ds(g, 1), :], 0.0).astype(jnp.bfloat16)
        w = lax.dot_general(ct_u[...], hot_u[...], NT, preferred_element_type=jnp.float32).astype(jnp.bfloat16)
        for d in range(3):
            for x in range(3):
                for c in range(3):
                    p = (d * 3 + x) * 3 + c
                    out_ref[x, 0, pl.ds(pl.multiple_of(c * T + g * G, G), G), d * WIN:(d + 1) * WIN] = w[p * G:(p + 1) * G, :]

    rounds = T // G // unroll

    def body(i, carry):
        for u in range(unroll):
            one_group(i * unroll + u, u)
        return carry

    lax.fori_loop(0, rounds, body, 0)


def make_operator(first, force, bond, nbr, counts, total_atoms, unroll=4):
    atoms = nbr.shape[1]
    blocks = atoms // T
    return pl.pallas_call(
        functools.partial(operator_kernel, total_atoms=total_atoms, unroll=unroll),
        grid_spec=pltpu.PrefetchScalarGridSpec(
            num_scalar_prefetch=1,
            grid=(blocks,),
            in_specs=[
                pl.BlockSpec((3, 3, 16, T), lambda s, f: (0, 0, 0, s)),
                pl.BlockSpec((3, 16, T), lambda s, f: (0, 0, s)),
                pl.BlockSpec((16, T), lambda s, f: (0, s)),
                pl.BlockSpec((1, T), lambda s, f: (0, s)),
            ],
            out_specs=pl.BlockSpec((3, 1, 3 * T, 3 * WIN), lambda s, f: (0, s, 0, 0)),
            scratch_shapes=[
                pltpu.VMEM((27, 8, 256), jnp.float32),
                pltpu.VMEM((8, 256), jnp.int32),
                pltpu.VMEM((unroll, WIN, 256), jnp.bfloat16),
                pltpu.VMEM((unroll, 27 * G, 256), jnp.bfloat16),
            ],
        ),
        out_shape=jax.ShapeDtypeStruct((3, blocks, 3 * T, 3 * WIN), jnp.bfloat16),
        compiler_params=pltpu.CompilerParams(vmem_limit_bytes=60 * 2**20),
        cost_estimate=cost(2 * 27 * atoms * WIN * 256, 2 * 27 * atoms * WIN),
        name="operator",
    )(first, force, bond, nbr, counts)


def fill(win, pieces):
    shards, _, width, _ = pieces[0][0].shape
    for m in range(shards):
        for d in range(3):
            at = d * WIN
            for ref, start, size in pieces:
                win[m * width:(m + 1) * width, at:at + size] = ref[m, d, :, pl.ds(start, size)]
                at += size


def flux_of(block, win):
    return lax.dot_general(block.reshape(9 * T, 3 * WIN), win[...], NT, preferred_element_type=jnp.float32).astype(jnp.bfloat16)


def keep_flux(flux, f, step):
    cols = f.shape[1]
    at = step % (S // T) * T
    for x in range(3):
        for c in range(3):
            flux[c * S + at:c * S + at + T, x * cols:(x + 1) * cols] = f[(x * 3 + c) * T:(x * 3 + c + 1) * T, :]


def middle_kernel(all_ref, main_ref, flux_ref, win, op, sems):
    step = pl.program_id(0)
    steps = op.shape[0]

    def fetch(e):
        return pltpu.make_async_copy(all_ref.at[:, e + REACH // T], op.at[e], sems.at[e])

    def one(e):
        if e == 0:
            for k in range(steps):
                fetch(k).start()
        fill(win, ((main_ref, e * T, WIN),))
        fetch(e).wait()
        keep_flux(flux_ref.at[e // (S // T)], flux_of(op[e], win), e)

    for e in range(steps):
        @pl.when(step == e)
        def _():
            one(e)


def middle(operator, main):
    shards, _, width, atoms = main.shape
    cols = shards * width
    inner = atoms - 2 * REACH
    return pl.pallas_call(
        middle_kernel,
        grid=(inner // T,),
        in_specs=[pl.BlockSpec(memory_space=pl.ANY), pl.BlockSpec(memory_space=pltpu.VMEM)],
        out_specs=pl.BlockSpec(memory_space=pltpu.VMEM),
        out_shape=pltpu.VMEM((inner // S, 3 * S, 3 * cols), jnp.bfloat16),
        scratch_shapes=[
            pltpu.VMEM((cols, 3 * WIN), jnp.bfloat16),
            pltpu.VMEM((inner // T, 3, 3 * T, 3 * WIN), jnp.bfloat16),
            pltpu.SemaphoreType.DMA((inner // T,)),
        ],
        compiler_params=pltpu.CompilerParams(vmem_limit_bytes=55 * 2**20),
        cost_estimate=cost(2 * inner * 9 * cols * 3 * WIN, 2 * inner * 9 * 3 * WIN),
        name="middle",
    )(operator, in_vmem(main))


def edges_kernel(core_ref, all_ref, left_ref, main_ref, low_ref, high_ref, mid_ref, keep_ref, send_ref, win, flux, acc, op, sems):
    step = pl.program_id(0)
    atoms = main_ref.shape[3]
    ends = REACH // T
    blocks = atoms // T
    slots = op.shape[0]

    def fetch(e):
        block = e if e < ends else e + blocks - 2 * ends
        return pltpu.make_async_copy(all_ref.at[:, block], op.at[e % slots], sems.at[e % slots])

    def add(fl):
        left = left_ref[...].reshape(3 * S, left_ref.shape[2])
        return lax.dot_general(left, fl, TN, preferred_element_type=jnp.float32)

    def one(e):
        if e + 2 < 2 * ends:
            fetch(e + 2).start()
        if e < ends:
            fill(win, ((low_ref, e * T, REACH - e * T), (main_ref, 0, WIN - REACH + e * T)))
        else:
            over = (e - ends + 1) * T
            fill(win, ((main_ref, atoms - WIN + over, WIN - over), (high_ref, 0, over)))
        fetch(e).wait()
        keep_flux(flux, flux_of(op[e % slots], win), e)

    @pl.when(step == 0)
    def _():
        fetch(0).start()
        acc[...] = add(mid_ref[0])

    @pl.when(step == 1)
    def _():
        fetch(1).start()
        acc[...] += add(mid_ref[1])

    for e in range(2 * ends):
        @pl.when(step == e + 2)
        def _():
            one(e)

    @pl.when(step == 3)
    def _():
        acc[...] += add(flux[...])

    @pl.when(step == 5)
    def _():
        acc[...] += add(flux[...])
        mine = send_ref.shape[1]
        core = core_ref[0]
        for q in range(send_ref.shape[0]):
            keep_ref[q] = acc[pl.ds(pl.multiple_of((2 * q + core) * mine, 8), mine), :]
            send_ref[q] = acc[pl.ds(pl.multiple_of((2 * q + 1 - core) * mine, 8), mine), :].astype(jnp.bfloat16)


def edges(core, operator, left, main, low, high, mid, chips):
    shards, _, width, atoms = main.shape
    cols = shards * width
    steps, modes = atoms // S, left.shape[2]
    ends = REACH // T
    slots = 2 * ends - 1
    half = (chips, modes // (2 * chips), 3 * cols)
    part = lambda b: jnp.where(b < 2, b + 1, jnp.where(b < 4, 0, steps - 1))
    return pl.pallas_call(
        edges_kernel,
        grid_spec=pltpu.PrefetchScalarGridSpec(
            num_scalar_prefetch=1,
            grid=(2 + 2 * ends,),
            in_specs=[
                pl.BlockSpec(memory_space=pl.ANY),
                pl.BlockSpec((3, S, modes), lambda b, s: (0, part(b), 0)),
            ]
            + [pl.BlockSpec(memory_space=pltpu.VMEM)] * 4,
            out_specs=[pl.BlockSpec(memory_space=pltpu.VMEM)] * 2,
            scratch_shapes=[
                pltpu.VMEM((cols, 3 * WIN), jnp.bfloat16),
                pltpu.VMEM((3 * S, 3 * cols), jnp.bfloat16),
                pltpu.VMEM((modes, 3 * cols), jnp.float32),
                pltpu.VMEM((slots, 3, 3 * T, 3 * WIN), jnp.bfloat16),
                pltpu.SemaphoreType.DMA((slots,)),
            ],
        ),
        out_shape=[pltpu.VMEM(half, jnp.float32), pltpu.VMEM(half, jnp.bfloat16)],
        compiler_params=pltpu.CompilerParams(vmem_limit_bytes=55 * 2**20),
        cost_estimate=cost(2 * 2 * REACH * 9 * cols * 3 * WIN + 2 * atoms * 9 * cols * modes, 2 * 2 * REACH * 9 * 3 * WIN),
        name="edges",
    )(core, operator, left, *[in_vmem(a) for a in (main, low, high, mid)])


omega_step = 0.05
gamma = 0.1


def per_device(left_modes, right_panel, force_blocks, bond_vectors, neighbours, counts, left_bins, right_bins):
    atoms_dev = right_panel.shape[1]
    cols = right_panel.shape[2]
    modes_dev = left_modes.shape[2]
    n_modes = lax.axis_size("modes")
    n_atoms = lax.axis_size("atoms")
    total_atoms = atoms_dev * n_atoms
    me = lax.axis_index("atoms")
    n_core = 2
    n_chip = n_atoms // n_core
    mine = modes_dev // n_atoms

    shard = jnp.swapaxes(right_panel, 1, 2)
    main = lax.all_to_all(spread(shard, n_modes), "modes", 0, 0, tiled=True)
    up = [(i, (i + 1) % n_atoms) for i in range(n_atoms)]
    down = [(i, (i - 1) % n_atoms) for i in range(n_atoms)]
    low = lax.ppermute(main[..., atoms_dev - REACH:], "atoms", up)
    high = lax.ppermute(main[..., :REACH], "atoms", down)

    first = (me * atoms_dev).astype(jnp.int32).reshape(1)
    core = (me % n_core).astype(jnp.int32).reshape(1)
    operator = make_operator(first, force_blocks, bond_vectors, neighbours, counts.reshape(1, -1), total_atoms, 8)
    mid = middle(operator, main)
    keep, send = edges(core, operator, left_modes, main, low, high, mid, n_chip)

    omega_left = omega_step * left_bins.astype(jnp.float32)
    omega_right = omega_step * right_bins.astype(jnp.float32)
    freq_gap = omega_left[:, None] - omega_right[None, :]
    weight = gamma * gamma / (freq_gap * freq_gap + gamma * gamma)
    weight = weight * (omega_left[:, None] + omega_right[None, :]) ** 2 / (4.0 * omega_left[:, None] * omega_right[None, :])
    weight = weight * (4.0 / (total_atoms * n_modes * cols))

    got = lax.ppermute(send, "atoms", [(i, i ^ 1) for i in range(n_atoms)])
    chip = (keep + got.astype(jnp.float32)).astype(jnp.bfloat16)
    groups = [[c + n_core * i for i in range(n_chip)] for c in range(n_core)]
    parts = lax.all_to_all(chip, "atoms", 0, 0, axis_index_groups=groups, tiled=True)
    width = weight.shape[1]
    total = jnp.sum(parts.astype(jnp.float32), axis=0)
    squares = sum(total[:, x * width:(x + 1) * width] ** 2 for x in range(3))
    return jnp.sum(weight * squares, axis=1)


def solution(mesh):
    from jax.sharding import PartitionSpec as P

    return jax.shard_map(
        per_device,
        mesh=mesh,
        in_specs=(
            P(None, "atoms", "modes"),
            P(None, "atoms", "modes"),
            P(None, None, None, "atoms"),
            P(None, None, "atoms"),
            P(None, "atoms"),
            P("atoms"),
            P(("modes", "atoms")),
            P(),
        ),
        out_specs=P(("modes", "atoms")),
        check_vma=False,
    )
```
